32 devices in a mesh: ctx: 8 (over y, x, core), head: 4 (over z).
Axes of the slice: x: 2, y: 2, z: 4, core: 2. Of those that a mesh axis runs over, the one named last changes fastest.
Arguments:
- queries: bfloat16 [2048, 4096], P(('ctx', 'head')), may hold values from -0.59765625 to 0.59765625
- key_in: bfloat16 [2048, 4096], P(('ctx', 'head')), may hold values from -0.59765625 to 0.59765625
- values_in: bfloat16 [2048, 4096], P(('ctx', 'head')), may hold values from -6 to 6
- strength: bfloat16 [2048, 32], P(('ctx', 'head')), may hold values from 0 to 0.95, as said below
- log_decay: bfloat16 [2048, 4096], P(('ctx', 'head')), may hold values from -1.2 to 0, as said below
- d_out: bfloat16 [2048, 4096], P(('ctx', 'head')), may hold values from -6 to 6
Outputs:
- d_queries: bfloat16 [2048, 4096], P(('ctx', 'head'))
- d_keys: bfloat16 [2048, 4096], P(('ctx', 'head'))
- d_values: bfloat16 [2048, 4096], P(('ctx', 'head'))
- d_strength: bfloat16 [2048, 32], P(('ctx', 'head'))
- d_log_decay: bfloat16 [2048, 4096], P(('ctx', 'head'))
The draws below stay inside these ranges and needn't reach their ends.
Inputs may be any that keep to these rules, and one draw needn't show every extreme that they name: `log_decay`: every log decay is negative. Every write strength is positive and below one.
All inputs are finite; a program needn't handle non-finite values.
Results may differ from the reference program's by a relative error of at most 0.00215.
Values may be sent and summed in bfloat16 or wider, within the bound.
A program may use at most 128 MiB of HBM per device.

```python
import jax
import jax.numpy as jnp
from jax import lax

HEADS = 32
HEAD_DIM = 128
SPAN = 64
TOK_CTX = 256
TOKENS = 2048


def draw_strength(key, part):
    shards = TOKENS // TOK_CTX
    pick_key, strong_key, weak_key, block_key, rough_key = jax.random.split(key, 5)
    share = 3
    strong_head = jax.random.randint(pick_key, (HEADS,), 0, 8) < share
    strong_value = jax.random.uniform(strong_key, (TOKENS, HEADS), jnp.float32, 0.2, 0.95)
    weak_base = jnp.exp(jax.random.uniform(weak_key, (HEADS,), jnp.float32, jnp.log(0.1), jnp.log(1.5))) * (HEAD_DIM / TOKENS)
    block_factor = jnp.exp(jax.random.uniform(block_key, (shards, 1, HEADS), jnp.float32, -0.7, 0.7))
    rough_factor = jnp.exp(jax.random.uniform(rough_key, (shards, TOK_CTX, HEADS), jnp.float32, -0.7, 0.7))
    weak_value = jnp.minimum((weak_base * block_factor * rough_factor).reshape(TOKENS, HEADS), 0.95)
    return jnp.where(strong_head[None, :], strong_value, weak_value).astype(jnp.bfloat16)


def draw_log_decay(key, part):
    channels = HEADS * HEAD_DIM
    shards = TOKENS // TOK_CTX
    pick_key, fast_key, slow_key, block_key, rough_key, spot_key, cut_key = jax.random.split(key, 7)
    share = 4
    fast_mask = jax.random.randint(pick_key, (channels,), 0, 8) < share
    fast_rate = jnp.exp(jax.random.uniform(fast_key, (channels,), jnp.float32, jnp.log(0.06), jnp.log(0.1)))
    slow_rate = jax.random.uniform(slow_key, (channels,), jnp.float32, 0.1, 1.0) * (1.0 / TOKENS)
    base_rate = jnp.where(fast_mask, fast_rate, slow_rate)
    block_factor = jnp.exp(jax.random.uniform(block_key, (shards, 1, channels), jnp.float32, -0.7, 0.7))
    rough_factor = jnp.exp(jax.random.uniform(rough_key, (shards, TOK_CTX, channels), jnp.float32, -0.7, 0.7))
    rates = (base_rate * block_factor * rough_factor).reshape(TOKENS, channels)
    spots = jax.random.randint(spot_key, (3,), 0, TOKENS)
    struck = jnp.any(jnp.arange(TOKENS)[:, None] == spots[None, :], axis=1)
    cuts = jnp.log(jax.random.uniform(cut_key, (TOKENS, channels), jnp.float32, 0.5, 0.8))
    return (jnp.where(struck[:, None], cuts, 0.0) - rates).astype(jnp.bfloat16)


def block_scale(rng, dims, cuts, least, top_value):
    def one(position, blocks):
        steps = jax.random.uniform(jax.random.fold_in(jax.random.fold_in(rng, 6), position), (blocks,), jnp.float32, least / len(cuts), top_value / len(cuts))
        return jnp.repeat(jnp.exp(steps), dims[position] // blocks).reshape((-1,) + (1,) * (len(dims) - position - 1))

    factor_of = one(*cuts[0])
    for cut in cuts[1:]:
        factor_of = factor_of * one(*cut)
    return factor_of


def gaussian(key, shape, width, bound, cuts=(), held_as=jnp.bfloat16):
    loudness = block_scale(key, shape, cuts, -0.22, 0.18) if cuts else 1.0
    values = jax.random.normal(key, shape, jnp.float32) * width * loudness
    return jnp.minimum(jnp.maximum(values, -bound), bound).astype(held_as)


def setup_inputs(seed: int = 0) -> dict:
    splits = jax.random.split(jax.random.key(seed), 7)
    queries = gaussian(splits[0], (TOKENS, HEADS * HEAD_DIM), 0.088, 0.59765625, ((0, 32),))
    key_in = gaussian(splits[1], (TOKENS, HEADS * HEAD_DIM), 0.088, 0.59765625, ((0, 32),))
    values_in = gaussian(splits[2], (TOKENS, HEADS * HEAD_DIM), 1.0, 6.0, ((0, 32),))
    strength = draw_strength(jax.random.fold_in(splits[6], 71), 0)
    log_decay = draw_log_decay(jax.random.fold_in(splits[6], 71), 0)
    d_out = gaussian(splits[5], (TOKENS, HEADS * HEAD_DIM), 1.0, 6.0, ((0, 32),))
    return {"queries": queries, "key_in": key_in, "values_in": values_in, "strength": strength, "log_decay": log_decay, "d_out": d_out}


exact_prec = lax.Precision.HIGHEST
epsilon = 1e-06

def prepare(queries, keys_used, values_used, strength, log_decay):
    span_len = queries.shape[1]
    head_width = queries.shape[3]
    q_unit = queries * lax.rsqrt(lax.optimization_barrier(jnp.sum(queries * queries, axis=3, keepdims=True)) + epsilon) * head_width ** (-0.5)
    k_unit = keys_used * lax.rsqrt(lax.optimization_barrier(jnp.sum(keys_used * keys_used, axis=3, keepdims=True)) + epsilon)
    gamma = jnp.cumsum(log_decay, axis=1)
    middle = gamma[:, span_len // 2 - 1:span_len // 2]
    q_rise = q_unit * jnp.exp(gamma - middle)
    k_rise = k_unit * jnp.exp(gamma - middle)
    k_fall = k_unit * jnp.exp(middle - gamma)
    strict_mask = jnp.tril(jnp.ones((span_len, span_len), jnp.float32), -1)
    causal_mask = jnp.tril(jnp.ones((span_len, span_len), jnp.float32))
    key_inner = jnp.einsum('ntha,nsha->nhts', k_rise, k_fall, precision=exact_prec) * strict_mask
    scores = jnp.einsum('ntha,nsha->nhts', q_rise, k_fall, precision=exact_prec) * causal_mask
    strength_t = jnp.transpose(strength, (0, 2, 1))
    system = jnp.eye(span_len, dtype=jnp.float32) + strength_t[..., None] * key_inner
    k_head = k_unit * jnp.exp(gamma)
    right_side = jnp.concatenate([values_used, k_head], axis=3) * strength[..., None]
    right_side = jnp.transpose(right_side, (0, 2, 1, 3))
    solved = lax.linalg.triangular_solve(system, right_side, left_side=True, lower=True, unit_diagonal=True)
    w_value = solved[..., :head_width]
    w_key = solved[..., head_width:]
    gamma_end = gamma[:, -1:]
    key_tail = k_unit * jnp.exp(gamma_end - gamma)
    fade_last = jnp.exp(gamma_end[:, 0])
    q_head = q_unit * jnp.exp(gamma)
    return (q_head, scores, w_value, w_key, key_tail, fade_last)

def march(w_value, w_key, key_tail, fade_last, state):

    def advance(state_now, piece_data):
        value_part, key_part, tail_part, fade_part = piece_data
        updates = value_part - jnp.einsum('hta,hab->htb', key_part, state_now, precision=exact_prec)
        following = fade_part[:, :, None] * state_now + jnp.einsum('tha,htb->hab', tail_part, updates, precision=exact_prec)
        return (following, (state_now, updates))
    final_state, (start_states, all_updates) = lax.scan(advance, state, (w_value, w_key, key_tail, fade_last))
    return (final_state, start_states, all_updates)

def sweep(prepared, state):
    q_head, scores, w_value, w_key, key_tail, fade_last = prepared
    final_state, start_states, all_updates = march(w_value, w_key, key_tail, fade_last, state)
    output = jnp.einsum('ntha,nhab->nthb', q_head, start_states, precision=exact_prec)
    output = output + jnp.einsum('nhts,nhsb->nthb', scores, all_updates, precision=exact_prec)
    return (output, final_state)

def reference(queries, key_in, values_in, strength, log_decay, d_out):
    heads_all = strength.shape[1]
    head_width = queries.shape[1] // heads_all
    total = queries.shape[0]
    blocks = total // SPAN

    def by_head(array):
        return jnp.transpose(array.reshape(total, heads_all, head_width), (1, 0, 2))

    def one_head(packed):
        q_one, k_one, v_one, s_one, g_one, o_one = packed

        def shaped(array):
            return array.astype(jnp.float32).reshape(blocks, SPAN, 1, head_width)

        def forward(q_in, k_in, v_in, s_in, g_in):
            prepared = prepare(q_in, k_in, v_in, s_in, g_in)
            return sweep(prepared, jnp.zeros((1, head_width, head_width), jnp.float32))[0]
        strength_one = s_one.astype(jnp.float32).reshape(blocks, SPAN, 1)
        _, pull = jax.vjp(forward, shaped(q_one), shaped(k_one), shaped(v_one), strength_one, shaped(g_one))
        d_q, d_k, d_v, d_s, d_g = pull(shaped(o_one))

        def flatten(array):
            return array.reshape(total, head_width).astype(jnp.bfloat16)
        return (flatten(d_q), flatten(d_k), flatten(d_v), d_s.reshape(total).astype(jnp.bfloat16), flatten(d_g))
    results = lax.map(one_head, (by_head(queries), by_head(key_in), by_head(values_in), jnp.transpose(strength), by_head(log_decay), by_head(d_out)))

    def regather(array):
        return jnp.transpose(array, (1, 0, 2)).reshape(total, heads_all * head_width)
    return (regather(results[0]), regather(results[1]), regather(results[2]), jnp.transpose(results[3]), regather(results[4]))
```

```python
import functools

import jax
import jax.numpy as jnp
from jax import lax
from jax.experimental import pallas as pl
from jax.experimental.pallas import tpu as pltpu
from jax.sharding import PartitionSpec as P

GROUP = 4
BASE = 8
TILE = 16
RANGE = 80.0
EPS = 1e-06
F32 = jnp.float32
BF16 = jnp.bfloat16
MESH = pl.DeviceIdType.MESH

NN = (((1,), (0,)), ((), ()))
NT = (((1,), (1,)), ((), ()))


def split(x):
    high = x.astype(BF16)
    return high, (x - high.astype(F32)).astype(BF16)


def mul(a, b, dims=NN):
    return lax.dot_general(a, b, dims, preferred_element_type=F32)


def dot3(a, b, dims=NN):
    if not isinstance(a, tuple):
        return mul(a, b[0], dims) + mul(a, b[1], dims)
    if not isinstance(b, tuple):
        return mul(a[0], b, dims) + mul(a[1], b, dims)
    return mul(a[0], b[0], dims) + (mul(a[0], b[1], dims) + mul(a[1], b[0], dims))


def dot32(a, b):
    return dot3(split(a), split(b))


def rows_of(pair, start, size):
    if not isinstance(pair, tuple):
        return pair[start : start + size]
    return tuple(part[start : start + size] for part in pair)


def grids(size):
    return (
        lax.broadcasted_iota(jnp.int32, (size, size), 0),
        lax.broadcasted_iota(jnp.int32, (size, size), 1),
    )


def code(x):
    top = jnp.max(jnp.abs(x), axis=0, keepdims=True)
    scale = (top * 1.01 + 1e-30).astype(BF16)
    return jnp.exp(x * (RANGE / scale.astype(F32))).astype(BF16), scale


def decode(pair):
    coded, scale = pair
    return jnp.log(coded.astype(F32)) * (scale.astype(F32) * (1.0 / RANGE))


def pack(ref, pairs):
    width = ref.shape[1]
    row = lax.broadcasted_iota(jnp.int32, (TILE, width), 0)
    scales = jnp.zeros((TILE, width), F32)
    for index, (coded, scale) in enumerate(pairs):
        ref[TILE + index * width : TILE + (index + 1) * width] = coded
        scales = jnp.where(row == index, scale.astype(F32), scales)
    ref[:TILE] = scales.astype(BF16)


def unpack(ref, index):
    width = ref.shape[1]
    scales = ref[:TILE].astype(F32)
    return ref[TILE + index * width : TILE + (index + 1) * width], scales[index : index + 1]


def per_span(row_values, span, like):
    rows, width = like.shape
    return jnp.broadcast_to(row_values, (rows // span, span, width)).reshape(rows, width)


def gates(g, span):
    rows, width = g.shape
    row, col = grids(rows)
    sum_mask = jnp.where((row // span == col // span) & (col <= row), 1.0, 0.0).astype(BF16)
    gamma = mul(sum_mask, g)
    spans = gamma.reshape(rows // span, span, width)
    middle = spans[:, span // 2 - 1 : span // 2]
    end = spans[:, span - 1 : span]
    centred = gamma - per_span(middle, span, gamma)
    rise = jnp.exp(centred)
    fall = jnp.exp(-centred)
    head = rise * per_span(jnp.exp(middle), span, gamma)
    tail = fall * per_span(jnp.exp(end - middle), span, gamma)
    fade = jnp.exp(end).reshape(rows // span, width)
    return rise, fall, head, tail, fade


def columns_of(table, first, count):
    heads, share = table.shape
    row, col = grids(share)
    head = lax.broadcasted_iota(jnp.int32, (heads, share), 0)
    lines = [jnp.sum(jnp.where(head == first + j, table, 0.0), axis=0, keepdims=True) for j in range(count)]
    return jnp.concatenate(
        [jnp.sum(jnp.where(row == col, line, 0.0), axis=1, keepdims=True) for line in lines], axis=0
    )


def norm_of(x):
    return lax.rsqrt(jnp.sum(x * x, axis=1, keepdims=True) + EPS)


def inverse(system, row, col, span):
    same = row // BASE == col // BASE
    near = jnp.where(same, system, 0.0)
    near_s = split(near)
    square = dot3(near_s, near_s)
    square_s = split(square)
    found = jnp.where(row == col, 1.0, 0.0) - near
    fourth = dot3(square_s, square_s)
    found = found + dot3(split(found), square_s)
    found = found + dot3(split(found), split(fourth))
    block = BASE
    while block < span:
        wide = row // (2 * block) == col // (2 * block)
        off = jnp.where(wide & (row // block != col // block), system, 0.0)
        found_s = split(found)
        found = found - dot3(found_s, split(dot3(split(off), found_s)))
        block *= 2
    return found


def loaded(held, g):
    count, share, width = held.shape[2:]
    return [held[index, g].reshape(count * share, width) for index in range(5)]


def local_part(g, held, table, saved, tags):
    ev_ref, ek_ref, inv_ref, a_ref, sc_ref = saved
    count, span, width = held.shape[2:]
    rows = count * span
    k, g_in, q, v, o = loaded(held, g)
    q = q.astype(F32)
    k = k.astype(F32)
    beta = columns_of(table[...].astype(F32), g * count, count)
    rise, fall, head, tail, fade = gates(g_in, span)
    q_unit = q * norm_of(q) * width ** (-0.5)
    k_unit = k * norm_of(k)
    row, col = grids(rows)
    inside = row // span == col // span
    k_fall_s = split(k_unit * fall)
    inner = jnp.where(inside & (col < row), dot3(split(k_unit * rise), k_fall_s, NT), 0.0)
    scores = jnp.where(inside & (col <= row), dot3(split(q_unit * rise), k_fall_s, NT), 0.0)
    a_ref[g] = inner
    sc_ref[g] = scores
    beta_row = jnp.sum(jnp.where(row == col, beta, 0.0), axis=0, keepdims=True)
    found = inverse(inner * beta_row, row, col, span)
    inv_ref[g] = found
    found_s = split(found)
    e_value = dot3(found_s, v)
    e_key = dot3(found_s, split(k_unit * head))
    ev_ref[g] = e_value
    ek_ref[g] = e_key
    w_key_s = split(e_key * beta)
    w_value_s = split(e_value * beta)
    reach = q_unit * head - dot3(split(scores), w_key_s)
    k_tail = k_unit * tail
    small_row, small_col = grids(width)
    diagonal = small_row == small_col
    for j in range(count):
        at = j * span
        tail_t = split(k_tail[at : at + span].T)
        tags[g, j, 0] = jnp.where(diagonal, fade[j : j + 1], 0.0) - dot3(tail_t, rows_of(w_key_s, at, span))
        tags[g, j, 1] = dot3(tail_t, rows_of(w_value_s, at, span))
        tags[g, j, 2] = dot3(split(reach[at : at + span].T), o[at : at + span])


def grad_part(g, held, table, saved, ends, db_all, emit_group):
    ev_ref, ek_ref, inv_ref, a_ref, sc_ref = saved
    count, span, width = held.shape[2:]
    rows = count * span
    k, g_in, q, _, o = loaded(held, g)
    q = q.astype(F32)
    k = k.astype(F32)
    beta = columns_of(table[...].astype(F32), g * count, count)

    def emit(index, value):
        emit_group(index, g, value)

    rise, fall, head, tail, fade = gates(g_in, span)
    q_norm = norm_of(q)
    k_norm = norm_of(k)
    q_unit = q * q_norm * width ** (-0.5)
    k_unit = k * k_norm
    row, col = grids(rows)
    inside = row // span == col // span
    states = [ends[g, j, 0] for j in range(count)]
    grads = [ends[g, j, 1] for j in range(count)]
    states_s = [split(x) for x in states]
    grads_s = [split(x) for x in grads]

    def each(fn):
        return jnp.concatenate([fn(index, index * span) for index in range(count)], axis=0)

    ek_s = split(ek_ref[g])
    k_tail = k_unit * tail
    k_tail_s = split(k_tail)
    error = ev_ref[g] - each(lambda i, at: dot3(rows_of(ek_s, at, span), states_s[i]))
    update_s = split(error * beta)
    d_update = dot3(split(sc_ref[g].T), o) + each(lambda i, at: dot3(rows_of(k_tail_s, at, span), grads_s[i]))
    d_value = dot3(split(inv_ref[g].T), split(d_update * beta))
    d_value_s = split(d_value)
    emit(0, d_value)
    residue = d_update - dot3(split(a_ref[g].T), d_value_s)
    d_beta = jnp.sum(error * residue, axis=1, keepdims=True)
    at_row, at_col = grids(span)
    sublane = lax.broadcasted_iota(jnp.int32, db_all.shape, 0)
    for j in range(count):
        piece = d_beta[j * span : (j + 1) * span]
        line = jnp.sum(jnp.where(at_row == at_col, piece, 0.0), axis=0, keepdims=True)
        db_all[...] = jnp.where(sublane == g * count + j, line, db_all[...])
    dq_head = each(lambda i, at: dot3(o[at : at + span], states_s[i], NT))
    dk_head = -each(lambda i, at: dot3(rows_of(d_value_s, at, span), states_s[i], NT))
    dk_tail = each(lambda i, at: dot3(rows_of(update_s, at, span), grads_s[i], NT))
    d_scores = jnp.where(inside & (col <= row), dot3(o, update_s, NT), 0.0)
    d_inner = jnp.where(inside & (col < row), -dot3(d_value_s, update_s, NT), 0.0)
    k_fall_s = split(k_unit * fall)
    dq_rise = dot3(split(d_scores), k_fall_s)
    dk_rise = dot3(split(d_inner), k_fall_s)
    dk_fall = dot3(split(d_scores.T), split(q_unit * rise)) + dot3(split(d_inner.T), split(k_unit * rise))
    dq_unit = dq_rise * rise + dq_head * head
    up = dk_rise * rise + dk_head * head
    tail_part = dk_tail * tail
    down = dk_fall * fall + tail_part
    d_gamma = q_unit * dq_unit + k_unit * (up - down)
    tail_sum = jnp.sum((k_unit * tail_part).reshape(count, span, width), axis=1, keepdims=True)
    small_row, small_col = grids(width)
    diagonal = small_row == small_col
    last = []
    for index in range(count):
        d_fade = jnp.sum(states[index] * grads[index], axis=1, keepdims=True)
        d_fade = jnp.sum(jnp.where(diagonal, d_fade, 0.0), axis=0, keepdims=True)
        last.append(d_fade * fade[index : index + 1])
    last = jnp.concatenate([x.reshape(1, 1, width) for x in last], axis=0)
    sum_mask = jnp.where(inside & (col >= row), 1.0, 0.0).astype(BF16)
    d_decay = dot3(sum_mask, split(d_gamma)) + per_span(tail_sum + last, span, d_gamma)
    scale = width ** (-0.5)
    dq = (dq_unit - q * (q_norm * q_norm * jnp.sum(q * dq_unit, axis=1, keepdims=True))) * (q_norm * scale)
    emit(1, dq)
    dk_unit = up + down
    dk = (dk_unit - k * (k_norm * k_norm * jnp.sum(k * dk_unit, axis=1, keepdims=True))) * k_norm
    emit(2, dk)
    emit(3, d_decay)


def merged(low, high):
    low_t, low_a, low_g = low
    high_t, high_a, high_g = high
    low_t_s, high_t_s = split(low_t), split(high_t)
    return (
        dot3(high_t_s, low_t_s),
        dot3(high_t_s, split(low_a)) + high_a,
        low_g + dot3(split(low_t.T), split(high_g)),
    )


def through(transfer, add, state):
    return dot32(transfer, state) + add


def through_back(transfer, add, grad):
    return dot32(transfer.T, grad) + add


def layer_kernel(n, rounds, q_ref, k_ref, v_ref, g_ref, o_ref, b_ref, dq_out, dk_out, dv_out, dg_out, db_out,
                 held, table, done, db_all, db_done, ev, ek, inv, a, sc, tags, ends, tot, lead, trail, state, dstate,
                 red_send, red_recv, back_send, back_recv, scan_send, scan_recv, last_send, last_recv,
                 in_sem, table_sem, out_sem, db_sem, red_sems, back_sems, scan_sems):
    t = pl.program_id(0)
    groups, count, span, width = held.shape[1:]
    half = count // 2
    ups = range(half, count)
    downs = range(half)
    z = lax.axis_index("head")
    me = lax.axis_index("ctx")
    above = lax.rem(z + 1, n)
    below = lax.rem(z + n - 1, n)
    saved = (ev, ek, inv, a, sc)
    ins = (k_ref, g_ref, q_ref, v_ref, o_ref)
    outs = (dv_out, dq_out, dk_out, dg_out)

    def columns(g, j):
        return pl.ds(pl.multiple_of((g * count + j) * width, width), width)

    def load(index, g, j):
        return pltpu.make_async_copy(ins[index].at[:, columns(g, j)], held.at[index, g, j], in_sem.at[g, index, j])

    def store(index, g, j):
        return pltpu.make_async_copy(done.at[index, g, j], outs[index].at[:, columns(g, j)], out_sem.at[g, index, j])

    def reduce_copy(g, j):
        return pltpu.make_async_remote_copy(
            src_ref=red_send.at[g, j], dst_ref=red_recv.at[g, j], send_sem=red_sems.at[0, g, j],
            recv_sem=red_sems.at[1, g, j], device_id={"head": above if j >= half else below}, device_id_type=MESH,
        )

    def back_copy(g, j):
        return pltpu.make_async_remote_copy(
            src_ref=back_send.at[g, j], dst_ref=back_recv.at[g, j], send_sem=back_sems.at[0, g, j],
            recv_sem=back_sems.at[1, g, j], device_id={"head": below if j >= half else above}, device_id_type=MESH,
        )

    def partner(r):
        bit = 2**r
        return me + bit - 2 * bit * lax.rem(me // bit, 2)

    def upper(r):
        return lax.rem(me // 2**r, 2) == 1

    def scan_copy(r, g, i):
        final = r == rounds - 1
        source, target = (last_send, last_recv) if final else (scan_send.at[r], scan_recv.at[r])
        return pltpu.make_async_remote_copy(
            src_ref=source.at[g, i], dst_ref=target.at[g, i], send_sem=scan_sems.at[0, r, g, i],
            recv_sem=scan_sems.at[1, r, g, i], device_id={"ctx": partner(r)}, device_id_type=MESH,
        )

    at_end = (z == 0) | (z == n - 1)

    @pl.when(t == 0)
    def _():
        def start_load(g, carry):
            for index in range(len(ins)):
                for j in range(count):
                    load(index, g, j).start()
            return carry

        lax.fori_loop(0, groups, start_load, 0)
        pltpu.make_async_copy(b_ref, table, table_sem).start()
        barrier = pltpu.get_barrier_semaphore()

        @pl.when(z > 0)
        def _():
            pl.semaphore_signal(barrier, inc=1, device_id={"head": below}, device_id_type=MESH)

        @pl.when(z < n - 1)
        def _():
            pl.semaphore_signal(barrier, inc=1, device_id={"head": above}, device_id_type=MESH)

        for r in range(rounds):
            pl.semaphore_signal(barrier, inc=1, device_id={"ctx": partner(r)}, device_id_type=MESH)
        db_all[...] = jnp.zeros_like(db_all)
        pl.semaphore_wait(barrier, rounds + jnp.where(z > 0, 1, 0) + jnp.where(z < n - 1, 1, 0))
        pltpu.make_async_copy(b_ref, table, table_sem).wait()

    def own(g, j):
        return tuple(tags[g, j, index] for index in range(3))

    def received(g, j):
        ref = red_recv.at[g, j]
        return tuple(decode(unpack(ref, index)) for index in range(3))

    def send_reduced(g, j, values):
        pack(red_send.at[g, j], [code(x) for x in values])
        reduce_copy(g, j).start()

    def begin_scan(g, i, values):
        for index in range(3):
            tot[g, i, index] = values[index]
        send_scan(0, g, i, values)

    def send_scan(r, g, i, values):
        if r < rounds - 1:
            pack(scan_send.at[r, g, i], [code(x) for x in values])
        else:
            pack(last_send.at[g, i], [code(jnp.where(upper(r), values[2], values[1]))])
        scan_copy(r, g, i).start()

    def local_stage(g):
        for index in range(len(ins)):
            for j in range(count):
                load(index, g, j).wait()
        local_part(g, held, table, saved, tags)

        @pl.when(z == 0)
        def _():
            for j in ups:
                send_reduced(g, j, own(g, j))

        @pl.when(z == n - 1)
        def _():
            for j in downs:
                send_reduced(g, j, own(g, j))

    def reduce_stage(s, g):
        @pl.when(z == s)
        def _():
            for j in ups:
                reduce_copy(g, j).wait_recv()
                values = merged(received(g, j), own(g, j))
                if s < n - 1:
                    send_reduced(g, j, values)
                else:
                    begin_scan(g, j - half, values)

        @pl.when(z == n - 1 - s)
        def _():
            for j in downs:
                reduce_copy(g, j).wait_recv()
                values = merged(own(g, j), received(g, j))
                if s < n - 1:
                    send_reduced(g, j, values)
                else:
                    begin_scan(g, j, values)

    def scan_stage(r, g):
        more = r < rounds - 1

        @pl.when(at_end & upper(r))
        def _():
            for i in range(half):
                scan_copy(r, g, i).wait_recv()
                if more:
                    ref = scan_recv.at[r, g, i]
                    other, other_ends, other_grad = (decode(unpack(ref, index)) for index in range(3))
                else:
                    other_ends = decode(unpack(last_recv.at[g, i], 0))
                if r == 0:
                    state[g, i] = other_ends
                    dstate[g, i] = jnp.zeros((width, width), F32)
                else:
                    lead_s = split(lead[g, i])
                    state[g, i] = state[g, i] + dot3(lead_s, split(other_ends))
                if more:
                    if r == 0:
                        lead[g, i] = other
                        row, col = grids(width)
                        trail[g, i] = jnp.where(row == col, 1.0, 0.0)
                    else:
                        lead[g, i] = dot3(lead_s, split(other))
                    values = merged((other, other_ends, other_grad), tuple(tot[g, i, index] for index in range(3)))
                    for index in range(3):
                        tot[g, i, index] = values[index]
                    send_scan(r + 1, g, i, values)

        @pl.when(at_end & jnp.logical_not(upper(r)))
        def _():
            for i in range(half):
                scan_copy(r, g, i).wait_recv()
                if more:
                    ref = scan_recv.at[r, g, i]
                    other, other_ends, other_grad = (decode(unpack(ref, index)) for index in range(3))
                else:
                    other_grad = decode(unpack(last_recv.at[g, i], 0))
                if r == 0:
                    dstate[g, i] = other_grad
                    state[g, i] = jnp.zeros((width, width), F32)
                else:
                    trail_s = split(trail[g, i])
                    dstate[g, i] = dstate[g, i] + dot3(trail_s, split(other_grad))
                if more:
                    if r == 0:
                        trail[g, i] = other.T
                        row, col = grids(width)
                        lead[g, i] = jnp.where(row == col, 1.0, 0.0)
                    else:
                        trail[g, i] = dot3(trail_s, split(other), NT)
                    values = merged(tuple(tot[g, i, index] for index in range(3)), (other, other_ends, other_grad))
                    for index in range(3):
                        tot[g, i, index] = values[index]
                    send_scan(r + 1, g, i, values)

        if not more:
            @pl.when(z == n - 1)
            def _():
                for j in ups:
                    give_up(g, j, n - 1, code(state[g, j - half]), code(dstate[g, j - half]),
                            state[g, j - half], dstate[g, j - half])

            @pl.when(z == 0)
            def _():
                for j in downs:
                    give_down(g, j, 0, code(state[g, j]), code(dstate[g, j]), state[g, j], dstate[g, j])

    def give_up(g, j, level, state_pair, grad_pair, state_now, grad_now):
        own_t, _, own_g = own(g, j)
        ends[g, j, 1] = grad_now
        if level > 0:
            low_t, low_a, _ = received(g, j)
            ends[g, j, 0] = through(low_t, low_a, state_now)
            pack(back_send.at[g, j], [state_pair, code(through_back(own_t, own_g, grad_now))])
            back_copy(g, j).start()
        else:
            ends[g, j, 0] = state_now

    def give_down(g, j, level, state_pair, grad_pair, state_now, grad_now):
        own_t, own_a, _ = own(g, j)
        ends[g, j, 0] = state_now
        if level < n - 1:
            high_t, _, high_g = received(g, j)
            ends[g, j, 1] = through_back(high_t, high_g, grad_now)
            pack(back_send.at[g, j], [code(through(own_t, own_a, state_now)), grad_pair])
            back_copy(g, j).start()
        else:
            ends[g, j, 1] = grad_now

    def back_stage(b, g):
        def taken(j):
            back_copy(g, j).wait_recv()
            ref = back_recv.at[g, j]
            pairs = [unpack(ref, index) for index in range(2)]
            return pairs + [decode(pair) for pair in pairs]

        @pl.when(z == n - 1 - b)
        def _():
            for j in ups:
                give_up(g, j, n - 1 - b, *taken(j))

        @pl.when(z == b)
        def _():
            for j in downs:
                give_down(g, j, b, *taken(j))

    def emit(index, g, value):
        done[index, g] = value.astype(BF16).reshape(count, span, width)
        for j in range(count):
            store(index, g, j).start()

    def at(delay, stage):
        g = t - delay

        @pl.when((g >= 0) & (g < groups))
        def _():
            stage(g)

    scan_at = n
    back_at = scan_at + rounds - 1
    grad_at = back_at + n
    at(0, local_stage)
    at(grad_at, lambda g: grad_part(g, held, table, saved, ends, db_all, emit))
    for b in range(n - 1, 0, -1):
        at(back_at + b, functools.partial(back_stage, b))
    for r in range(rounds - 1, -1, -1):
        at(scan_at + r, functools.partial(scan_stage, r))
    for s in range(n - 1, 0, -1):
        at(s, functools.partial(reduce_stage, s))

    @pl.when(t == groups + grad_at - 1)
    def _():
        db_done[...] = db_all[...].astype(BF16)
        db_copy = pltpu.make_async_copy(db_done, db_out, db_sem)
        db_copy.start()

        def finish(g, carry):
            for index in range(len(outs)):
                for j in range(count):
                    store(index, g, j).wait()

            @pl.when(z < n - 1)
            def _():
                for j in ups:
                    reduce_copy(g, j).wait_send()
                for j in downs:
                    back_copy(g, j).wait_send()

            @pl.when(z > 0)
            def _():
                for j in downs:
                    reduce_copy(g, j).wait_send()
                for j in ups:
                    back_copy(g, j).wait_send()

            @pl.when(at_end)
            def _():
                for r in range(rounds):
                    for i in range(half):
                        scan_copy(r, g, i).wait_send()

            return carry

        lax.fori_loop(0, groups, finish, 0)
        db_copy.wait()


def per_device(queries, key_in, values_in, strength, log_decay, d_out):
    share, heads = strength.shape
    n = lax.axis_size("head")
    rounds = lax.axis_size("ctx").bit_length() - 1
    width = queries.shape[1] // heads
    count = GROUP
    half = count // 2
    groups = heads // count
    rows = count * share
    outside = pl.BlockSpec(memory_space=pl.ANY)
    full_t = jax.ShapeDtypeStruct(queries.shape, BF16)
    dma = pltpu.SemaphoreType.DMA
    vmem = pltpu.VMEM
    narrow = vmem((groups, rows, width), F32)
    square = vmem((groups, rows, rows), F32)
    state = vmem((groups, half, width, width), F32)
    reduced = vmem((groups, count, TILE + 3 * width, width), BF16)
    returned = vmem((groups, count, TILE + 2 * width, width), BF16)
    scanned = vmem((max(rounds - 1, 1), groups, half, TILE + 3 * width, width), BF16)
    final = vmem((groups, half, TILE + width, width), BF16)
    steps = groups + n + rounds - 1 + n
    dq, dk, dv, dg, ds = pl.pallas_call(
        functools.partial(layer_kernel, n, rounds),
        grid=(steps,),
        in_specs=[outside] * 6,
        out_specs=[outside] * 5,
        out_shape=[full_t] * 4 + [jax.ShapeDtypeStruct((heads, share), BF16)],
        scratch_shapes=[
            vmem((5, groups, count, share, width), BF16), vmem((heads, share), BF16),
            vmem((4, groups, count, share, width), BF16), vmem((heads, share), F32), vmem((heads, share), BF16),
        ] + [narrow] * 2 + [square] * 3 + [
            vmem((groups, count, 3, width, width), F32), vmem((groups, count, 2, width, width), F32),
            vmem((groups, half, 3, width, width), F32),
        ] + [state] * 4 + [reduced] * 2 + [returned] * 2 + [scanned] * 2 + [final] * 2 + [
            dma((groups, 5, count)), dma(()), dma((groups, 4, count)), dma(()),
            dma((2, groups, count)), dma((2, groups, count)), dma((2, rounds, groups, half)),
        ],
        compiler_params=pltpu.CompilerParams(
            dimension_semantics=("arbitrary",), vmem_limit_bytes=63 * 1024 * 1024,
            collective_id=0, has_side_effects=True,
        ),
        name="layer",
    )(queries, key_in, values_in, log_decay, d_out, strength.T)
    return dq, dk, dv, ds.T, dg


def solution(mesh):
    spec = P(("ctx", "head"), None)
    return jax.shard_map(
        per_device, mesh=mesh, in_specs=(spec,) * 6, out_specs=(spec,) * 5, check_vma=False
    )
```

```python
import functools

import jax
import jax.numpy as jnp
from jax import lax
from jax.experimental import pallas as pl
from jax.experimental.pallas import tpu as pltpu
from jax.sharding import PartitionSpec as P

GROUP = 2
HOP = 3
SWAP = 4
NEAR = 2
EVERY = 2
BACK = 4
BATCH = 4
BASE = 2
TILE = 16
RANGE = 80.0
EPS = 1e-06
F32 = jnp.float32
BF16 = jnp.bfloat16
MESH = pl.DeviceIdType.MESH

NN = (((1,), (0,)), ((), ()))
NT = (((1,), (1,)), ((), ()))


def split(x):
    high = x.astype(BF16)
    return high, (x - high.astype(F32)).astype(BF16)


def mul(a, b, dims=NN):
    return lax.dot_general(a, b, dims, preferred_element_type=F32)


def dot3(a, b, dims=NN):
    if not isinstance(a, tuple):
        return mul(a, b[0], dims) + mul(a, b[1], dims)
    if not isinstance(b, tuple):
        return mul(a[0], b, dims) + mul(a[1], b, dims)
    return mul(a[0], b[0], dims) + (mul(a[0], b[1], dims) + mul(a[1], b[0], dims))


def dot32(a, b):
    return dot3(split(a), split(b))


def rows_of(pair, start, size):
    if not isinstance(pair, tuple):
        return pair[start : start + size]
    return tuple(part[start : start + size] for part in pair)


def grids(size):
    return (
        lax.broadcasted_iota(jnp.int32, (size, size), 0),
        lax.broadcasted_iota(jnp.int32, (size, size), 1),
    )


def code(x):
    top = jnp.max(jnp.abs(x), axis=0, keepdims=True)
    scale = (top * 1.01 + 1e-30).astype(BF16)
    return jnp.exp(x * (RANGE / scale.astype(F32))).astype(BF16), scale


def decode(pair):
    coded, scale = pair
    return jnp.log(coded.astype(F32)) * (scale.astype(F32) * (1.0 / RANGE))


def pack(ref, pairs):
    width = ref.shape[1]
    row = lax.broadcasted_iota(jnp.int32, (TILE, width), 0)
    scales = jnp.zeros((TILE, width), F32)
    for index, (coded, scale) in enumerate(pairs):
        ref[TILE + index * width : TILE + (index + 1) * width] = coded
        scales = jnp.where(row == index, scale.astype(F32), scales)
    ref[:TILE] = scales.astype(BF16)


def unpack(ref, index):
    width = ref.shape[1]
    scales = ref[:TILE].astype(F32)
    return ref[TILE + index * width : TILE + (index + 1) * width], scales[index : index + 1]


def per_span(row_values, span, like):
    rows, width = like.shape
    return jnp.broadcast_to(row_values, (rows // span, span, width)).reshape(rows, width)


def gates(g, span):
    rows, width = g.shape
    row, col = grids(rows)
    sum_mask = jnp.where((row // span == col // span) & (col <= row), 1.0, 0.0).astype(BF16)
    gamma = mul(sum_mask, g)
    spans = gamma.reshape(rows // span, span, width)
    middle = spans[:, span // 2 - 1 : span // 2]
    end = spans[:, span - 1 : span]
    centred = gamma - per_span(middle, span, gamma)
    rise = jnp.exp(centred)
    fall = jnp.exp(-centred)
    head = rise * per_span(jnp.exp(middle), span, gamma)
    tail = fall * per_span(jnp.exp(end - middle), span, gamma)
    fade = jnp.exp(end).reshape(rows // span, width)
    return rise, fall, head, tail, fade


def columns_of(table, first, count):
    heads, share = table.shape
    row, col = grids(share)
    head = lax.broadcasted_iota(jnp.int32, (heads, share), 0)
    lines = [jnp.sum(jnp.where(head == first + j, table, 0.0), axis=0, keepdims=True) for j in range(count)]
    return jnp.concatenate(
        [jnp.sum(jnp.where(row == col, line, 0.0), axis=1, keepdims=True) for line in lines], axis=0
    )


def norm_of(x):
    return lax.rsqrt(jnp.sum(x * x, axis=1, keepdims=True) + EPS)


def inverses(systems, row, col, span):
    unit = jnp.where(row == col, 1.0, 0.0)
    founds = [unit - jnp.where(row // BASE == col // BASE, x, 0.0) for x in systems]
    block = BASE
    while block < span:
        off = (row // (2 * block) == col // (2 * block)) & (row // block != col // block)
        lows = [x.astype(BF16) for x in founds]
        inner = [mul(jnp.where(off, x, 0.0).astype(BF16), y) for x, y in zip(systems, lows)]
        founds = [x - mul(y, z.astype(BF16)) for x, y, z in zip(founds, lows, inner)]
        block *= 2
    lows = [x.astype(BF16) for x in founds]
    rests = [unit - y.astype(F32) - dot3(split(x), y) for x, y in zip(systems, lows)]
    small = [x.astype(BF16) for x in rests]
    rests = [x + mul(y, y) for x, y in zip(rests, small)]
    return [y.astype(F32) + mul(y, x.astype(BF16)) for x, y in zip(rests, lows)]


def loaded(held, index, batch, units, count):
    width = held.shape[3] // (units * count)

    def head(h):
        return held[index, batch, :, h * width : (h + 1) * width]

    return [jnp.concatenate([head(u * count + j) for j in range(count)], axis=0) for u in range(units)]


def over(fn, *lists):
    return [fn(*values) for values in zip(*lists)]


def local_part(batch, units, count, held, table, saved, tags):
    ev_ref, ek_ref, inv_ref, a_ref, sc_ref = saved
    span = held.shape[2]
    width = held.shape[3] // (units * count)
    rows = count * span
    first = batch * units
    ks, gs, qs, vs, os = (loaded(held, index, batch, units, count) for index in range(5))
    betas = columns_of(table[...].astype(F32), first * count, units * count)
    betas = [betas[u * rows : (u + 1) * rows] for u in range(units)]
    qs = over(lambda x: x.astype(F32), qs)
    ks = over(lambda x: x.astype(F32), ks)
    rises, falls, heads, tails, fades = zip(*(gates(x, span) for x in gs))
    q_units = over(lambda q: q * norm_of(q) * width ** (-0.5), qs)
    k_units = over(lambda k: k * norm_of(k), ks)
    row, col = grids(rows)
    inside = row // span == col // span
    k_falls = over(lambda k, fall: split(k * fall), k_units, falls)
    inners = over(
        lambda k, rise, k_fall: jnp.where(inside & (col < row), dot3(split(k * rise), k_fall, NT), 0.0),
        k_units, rises, k_falls,
    )
    beta_rows = over(lambda x: jnp.sum(jnp.where(row == col, x, 0.0), axis=0, keepdims=True), betas)
    systems = over(lambda inner, beta: inner * beta, inners, beta_rows)
    scores = over(
        lambda q, rise, k_fall: jnp.where(inside & (col <= row), dot3(split(q * rise), k_fall, NT), 0.0),
        q_units, rises, k_falls,
    )
    founds = inverses(systems, row, col, span)
    founds_s = over(split, founds)
    e_keys = over(lambda x, k, head: dot3(x, split(k * head)), founds_s, k_units, heads)
    e_values = over(dot3, founds_s, vs)
    w_keys = over(lambda x, beta: split(x * beta), e_keys, betas)
    w_values = over(lambda x, beta: split(x * beta), e_values, betas)
    reaches = over(lambda q, head, score, w: q * head - dot3(split(score), w), q_units, heads, scores, w_keys)
    k_tails = over(lambda k, tail: k * tail, k_units, tails)
    small_row, small_col = grids(width)
    diagonal = small_row == small_col
    for u in range(units):
        g = first + u
        a_ref[g] = inners[u]
        sc_ref[g] = scores[u]
        inv_ref[g] = founds[u]
        ev_ref[g] = e_values[u]
        ek_ref[g] = e_keys[u]
    for j in range(count):
        at = j * span
        tails_t = over(lambda x: split(x[at : at + span].T), k_tails)
        reaches_t = over(lambda x: split(x[at : at + span].T), reaches)
        for u in range(units):
            g = first + u
            tags[g, j, 0] = jnp.where(diagonal, fades[u][j : j + 1], 0.0) - dot3(tails_t[u], rows_of(w_keys[u], at, span))
            tags[g, j, 1] = dot3(tails_t[u], rows_of(w_values[u], at, span))
            tags[g, j, 2] = dot3(reaches_t[u], os[u][at : at + span])


def grad_part(batch, units, count, held, table, saved, ends, db_all, done):
    ev_ref, ek_ref, inv_ref, a_ref, sc_ref = saved
    span = held.shape[2]
    width = held.shape[3] // (units * count)
    rows = count * span
    first = batch * units
    spans = range(count)
    ks, gs, qs, _, os = (loaded(held, index, batch, units, count) for index in range(5))
    betas = columns_of(table[...].astype(F32), first * count, units * count)
    betas = [betas[u * rows : (u + 1) * rows] for u in range(units)]
    numbers = [first + u for u in range(units)]
    states = [[ends[g, j, 0] for j in spans] for g in numbers]
    grads = [[ends[g, j, 1] for j in spans] for g in numbers]
    scores_t = [sc_ref[g].T for g in numbers]
    inner_t = [a_ref[g].T for g in numbers]
    found_t = [inv_ref[g].T for g in numbers]
    e_values = [ev_ref[g] for g in numbers]
    e_keys = [ek_ref[g] for g in numbers]

    def emit(index, values):
        for u, value in enumerate(values):
            for j in spans:
                at = (u * count + j) * width
                done[index, batch, :, at : at + width] = value[j * span : (j + 1) * span].astype(BF16)

    qs = over(lambda x: x.astype(F32), qs)
    ks = over(lambda x: x.astype(F32), ks)
    rises, falls, heads, tails, fades = zip(*(gates(x, span) for x in gs))
    q_norms = over(norm_of, qs)
    k_norms = over(norm_of, ks)
    q_units = over(lambda q, norm: q * norm * width ** (-0.5), qs, q_norms)
    k_units = over(lambda k, norm: k * norm, ks, k_norms)
    row, col = grids(rows)
    inside = row // span == col // span
    states_s = [over(split, x) for x in states]
    grads_s = [over(split, x) for x in grads]

    def each(fn):
        return jnp.concatenate([fn(j, j * span) for j in spans], axis=0)

    def cut(x, at):
        return rows_of(x, at, span)

    e_keys = over(split, e_keys)
    k_tails = over(lambda k, tail: split(k * tail), k_units, tails)
    errors = over(lambda ev, ek, state: ev - each(lambda j, at: dot3(cut(ek, at), state[j])), e_values, e_keys, states_s)
    updates = over(lambda x, beta: split(x * beta), errors, betas)
    d_updates = over(
        lambda score, o, tail, grad: dot3(split(score), o) + each(lambda j, at: dot3(cut(tail, at), grad[j])),
        scores_t, os, k_tails, grads_s,
    )
    d_values = over(lambda x, d, beta: dot3(split(x), split(d * beta)), found_t, d_updates, betas)
    emit(0, d_values)
    d_values = over(split, d_values)
    residues = over(lambda d, a, value: d - dot3(split(a), value), d_updates, inner_t, d_values)
    d_betas = over(lambda x, y: jnp.sum(x * y, axis=1, keepdims=True), errors, residues)
    at_row, at_col = grids(span)
    sublane = lax.broadcasted_iota(jnp.int32, db_all.shape, 0)
    table_now = db_all[...]
    for u in range(units):
        for j in spans:
            piece = d_betas[u][j * span : (j + 1) * span]
            line = jnp.sum(jnp.where(at_row == at_col, piece, 0.0), axis=0, keepdims=True)
            table_now = jnp.where(sublane == (first + u) * count + j, line, table_now)
    db_all[...] = table_now
    dq_heads = over(lambda o, state: each(lambda j, at: dot3(cut(o, at), state[j], NT)), os, states_s)
    dk_heads = over(lambda d, state: -each(lambda j, at: dot3(cut(d, at), state[j], NT)), d_values, states_s)
    dk_tails = over(lambda x, grad: each(lambda j, at: dot3(cut(x, at), grad[j], NT)), updates, grads_s)
    d_scores = over(lambda o, x: jnp.where(inside & (col <= row), dot3(o, x, NT), 0.0), os, updates)
    d_inners = over(lambda d, x: jnp.where(inside & (col < row), -dot3(d, x, NT), 0.0), d_values, updates)
    k_falls = over(lambda k, fall: split(k * fall), k_units, falls)
    dq_rises = over(lambda x, y: dot3(split(x), y), d_scores, k_falls)
    dk_rises = over(lambda x, y: dot3(split(x), y), d_inners, k_falls)
    dk_falls = over(
        lambda x, y, q, k, rise: dot3(split(x.T), split(q * rise)) + dot3(split(y.T), split(k * rise)),
        d_scores, d_inners, q_units, k_units, rises,
    )
    dq_units = over(lambda x, rise, y, head: x * rise + y * head, dq_rises, rises, dq_heads, heads)
    ups = over(lambda x, rise, y, head: x * rise + y * head, dk_rises, rises, dk_heads, heads)
    tail_parts = over(lambda x, tail: x * tail, dk_tails, tails)
    downs = over(lambda x, fall, y: x * fall + y, dk_falls, falls, tail_parts)
    d_gammas = over(lambda q, dq, k, up, down: q * dq + k * (up - down), q_units, dq_units, k_units, ups, downs)
    tail_sums = over(lambda k, x: jnp.sum((k * x).reshape(count, span, width), axis=1, keepdims=True), k_units, tail_parts)
    small_row, small_col = grids(width)
    diagonal = small_row == small_col

    def at_last(state, grad, fade):
        last = []
        for j in spans:
            d_fade = jnp.sum(state[j] * grad[j], axis=1, keepdims=True)
            d_fade = jnp.sum(jnp.where(diagonal, d_fade, 0.0), axis=0, keepdims=True)
            last.append((d_fade * fade[j : j + 1]).reshape(1, 1, width))
        return jnp.concatenate(last, axis=0)

    lasts = over(at_last, states, grads, fades)
    sum_mask = jnp.where(inside & (col >= row), 1.0, 0.0).astype(BF16)
    d_decays = over(
        lambda x, tail, last: dot3(sum_mask, split(x)) + per_span(tail + last, span, x), d_gammas, tail_sums, lasts
    )
    scale = width ** (-0.5)
    emit(1, over(
        lambda d, q, norm: (d - q * (norm * norm * jnp.sum(q * d, axis=1, keepdims=True))) * (norm * scale),
        dq_units, qs, q_norms,
    ))
    dk_units = over(lambda x, y: x + y, ups, downs)
    emit(2, over(
        lambda d, k, norm: (d - k * (norm * norm * jnp.sum(k * d, axis=1, keepdims=True))) * norm,
        dk_units, ks, k_norms,
    ))
    emit(3, d_decays)


def merged(low, high):
    low_t, low_a, low_g = low
    high_t, high_a, high_g = high
    low_t_s, high_t_s = split(low_t), split(high_t)
    return (
        dot3(high_t_s, low_t_s),
        dot3(high_t_s, split(low_a)) + high_a,
        low_g + dot3(split(low_t.T), split(high_g)),
    )


def through(transfer, add, state):
    return dot32(transfer, state) + add


def through_back(transfer, add, grad):
    return dot32(transfer.T, grad) + add


def schedule(n, rounds):
    reduce_at = [HOP * s for s in range(n)]
    scan_at = []
    for r in range(rounds):
        near = r == 0 or r == rounds - 1
        scan_at.append((scan_at[-1] if r else reduce_at[-1]) + (NEAR if near else SWAP))
    back_at = [scan_at[-1] + BACK * b for b in range(n)]
    return reduce_at, scan_at, back_at, back_at[-1] + 1


def layer_kernel(n, rounds, q_ref, k_ref, v_ref, g_ref, o_ref, b_ref, dq_out, dk_out, dv_out, dg_out, db_out,
                 held, table, done, db_all, db_done, ev, ek, inv, a, sc, tags, ends, tot, lead, trail, state, dstate,
                 red_send, red_recv, back_send, back_recv, scan_send, scan_recv, last_send, last_recv,
                 in_sem, table_sem, out_sem, db_sem, red_sems, back_sems, scan_sems):
    t = pl.program_id(0)
    groups, count, _, width, _ = tags.shape
    batches = held.shape[1]
    units = groups // batches
    half = count // 2
    ups = range(half, count)
    downs = range(half)
    z = lax.axis_index("head")
    me = lax.axis_index("ctx")
    above = lax.rem(z + 1, n)
    below = lax.rem(z + n - 1, n)
    saved = (ev, ek, inv, a, sc)
    ins = (k_ref, g_ref, q_ref, v_ref, o_ref)
    outs = (dv_out, dq_out, dk_out, dg_out)

    def columns(batch):
        size = units * count * width
        return pl.ds(pl.multiple_of(batch * size, size), size)

    def load(index, batch):
        return pltpu.make_async_copy(ins[index].at[:, columns(batch)], held.at[index, batch], in_sem.at[batch, index])

    def store(index, batch):
        return pltpu.make_async_copy(done.at[index, batch], outs[index].at[:, columns(batch)], out_sem.at[batch, index])

    def reduce_copy(g, j):
        return pltpu.make_async_remote_copy(
            src_ref=red_send.at[g, j], dst_ref=red_recv.at[g, j], send_sem=red_sems.at[0, g, j],
            recv_sem=red_sems.at[1, g, j], device_id={"head": above if j >= half else below}, device_id_type=MESH,
        )

    def back_copy(g, j):
        return pltpu.make_async_remote_copy(
            src_ref=back_send.at[g, j], dst_ref=back_recv.at[g, j], send_sem=back_sems.at[0, g, j],
            recv_sem=back_sems.at[1, g, j], device_id={"head": below if j >= half else above}, device_id_type=MESH,
        )

    def partner(r):
        bit = 2**r
        return me + bit - 2 * bit * lax.rem(me // bit, 2)

    def upper(r):
        return lax.rem(me // 2**r, 2) == 1

    def scan_copy(r, g, i):
        final = r == rounds - 1
        source, target = (last_send, last_recv) if final else (scan_send.at[r], scan_recv.at[r])
        return pltpu.make_async_remote_copy(
            src_ref=source.at[g, i], dst_ref=target.at[g, i], send_sem=scan_sems.at[0, r, g, i],
            recv_sem=scan_sems.at[1, r, g, i], device_id={"ctx": partner(r)}, device_id_type=MESH,
        )

    at_end = (z == 0) | (z == n - 1)

    @pl.when(t == 0)
    def _():
        def start_load(batch, carry):
            for index in range(len(ins)):
                load(index, batch).start()
            return carry

        lax.fori_loop(0, batches, start_load, 0)
        pltpu.make_async_copy(b_ref, table, table_sem).start()
        barrier = pltpu.get_barrier_semaphore()

        @pl.when(z > 0)
        def _():
            pl.semaphore_signal(barrier, inc=1, device_id={"head": below}, device_id_type=MESH)

        @pl.when(z < n - 1)
        def _():
            pl.semaphore_signal(barrier, inc=1, device_id={"head": above}, device_id_type=MESH)

        for r in range(rounds):
            pl.semaphore_signal(barrier, inc=1, device_id={"ctx": partner(r)}, device_id_type=MESH)
        db_all[...] = jnp.zeros_like(db_all)
        pl.semaphore_wait(barrier, rounds + jnp.where(z > 0, 1, 0) + jnp.where(z < n - 1, 1, 0))
        pltpu.make_async_copy(b_ref, table, table_sem).wait()

    def own(g, j):
        return tuple(tags[g, j, index] for index in range(3))

    def received(g, j):
        ref = red_recv.at[g, j]
        return tuple(decode(unpack(ref, index)) for index in range(3))

    def send_reduced(g, j, values):
        pack(red_send.at[g, j], [code(x) for x in values])
        reduce_copy(g, j).start()

    def begin_scan(g, i, values):
        for index in range(3):
            tot[g, i, index] = values[index]
        send_scan(0, g, i, values)

    def send_scan(r, g, i, values):
        if r < rounds - 1:
            pack(scan_send.at[r, g, i], [code(x) for x in values])
        else:
            pack(last_send.at[g, i], [code(jnp.where(upper(r), values[2], values[1]))])
        scan_copy(r, g, i).start()

    def local_stage(batch):
        for index in range(len(ins)):
            load(index, batch).wait()
        local_part(batch, units, count, held, table, saved, tags)

        @pl.when(z == 0)
        def _():
            for u in range(units):
                for j in ups:
                    send_reduced(batch * units + u, j, own(batch * units + u, j))

        @pl.when(z == n - 1)
        def _():
            for u in range(units):
                for j in downs:
                    send_reduced(batch * units + u, j, own(batch * units + u, j))

    def grad_stage(batch):
        grad_part(batch, units, count, held, table, saved, ends, db_all, done)
        for index in range(len(outs)):
            store(index, batch).start()

    def reduce_stage(s, g):
        @pl.when(z == s)
        def _():
            for j in ups:
                reduce_copy(g, j).wait_recv()
                values = merged(received(g, j), own(g, j))
                if s < n - 1:
                    send_reduced(g, j, values)
                else:
                    begin_scan(g, j - half, values)

        @pl.when(z == n - 1 - s)
        def _():
            for j in downs:
                reduce_copy(g, j).wait_recv()
                values = merged(own(g, j), received(g, j))
                if s < n - 1:
                    send_reduced(g, j, values)
                else:
                    begin_scan(g, j, values)

    def scan_stage(r, g):
        more = r < rounds - 1

        @pl.when(at_end & upper(r))
        def _():
            for i in range(half):
                scan_copy(r, g, i).wait_recv()
                if more:
                    ref = scan_recv.at[r, g, i]
                    other, other_ends, other_grad = (decode(unpack(ref, index)) for index in range(3))
                else:
                    other_ends = decode(unpack(last_recv.at[g, i], 0))
                if r == 0:
                    state[g, i] = other_ends
                    dstate[g, i] = jnp.zeros((width, width), F32)
                else:
                    lead_s = split(lead[g, i])
                    state[g, i] = state[g, i] + dot3(lead_s, split(other_ends))
                if more:
                    if r == 0:
                        lead[g, i] = other
                        row, col = grids(width)
                        trail[g, i] = jnp.where(row == col, 1.0, 0.0)
                    else:
                        lead[g, i] = dot3(lead_s, split(other))
                    values = merged((other, other_ends, other_grad), tuple(tot[g, i, index] for index in range(3)))
                    for index in range(3):
                        tot[g, i, index] = values[index]
                    send_scan(r + 1, g, i, values)

        @pl.when(at_end & jnp.logical_not(upper(r)))
        def _():
            for i in range(half):
                scan_copy(r, g, i).wait_recv()
                if more:
                    ref = scan_recv.at[r, g, i]
                    other, other_ends, other_grad = (decode(unpack(ref, index)) for index in range(3))
                else:
                    other_grad = decode(unpack(last_recv.at[g, i], 0))
                if r == 0:
                    dstate[g, i] = other_grad
                    state[g, i] = jnp.zeros((width, width), F32)
                else:
                    trail_s = split(trail[g, i])
                    dstate[g, i] = dstate[g, i] + dot3(trail_s, split(other_grad))
                if more:
                    if r == 0:
                        trail[g, i] = other.T
                        row, col = grids(width)
                        lead[g, i] = jnp.where(row == col, 1.0, 0.0)
                    else:
                        trail[g, i] = dot3(trail_s, split(other), NT)
                    values = merged(tuple(tot[g, i, index] for index in range(3)), (other, other_ends, other_grad))
                    for index in range(3):
                        tot[g, i, index] = values[index]
                    send_scan(r + 1, g, i, values)

        if not more:
            @pl.when(z == n - 1)
            def _():
                for j in ups:
                    give_up(g, j, n - 1, code(state[g, j - half]), code(dstate[g, j - half]),
                            state[g, j - half], dstate[g, j - half])

            @pl.when(z == 0)
            def _():
                for j in downs:
                    give_down(g, j, 0, code(state[g, j]), code(dstate[g, j]), state[g, j], dstate[g, j])

    def give_up(g, j, level, state_pair, grad_pair, state_now, grad_now):
        own_t, _, own_g = own(g, j)
        ends[g, j, 1] = grad_now
        if level > 0:
            low_t, low_a, _ = received(g, j)
            ends[g, j, 0] = through(low_t, low_a, state_now)
            pack(back_send.at[g, j], [state_pair, code(through_back(own_t, own_g, grad_now))])
            back_copy(g, j).start()
        else:
            ends[g, j, 0] = state_now

    def give_down(g, j, level, state_pair, grad_pair, state_now, grad_now):
        own_t, own_a, _ = own(g, j)
        ends[g, j, 0] = state_now
        if level < n - 1:
            high_t, _, high_g = received(g, j)
            ends[g, j, 1] = through_back(high_t, high_g, grad_now)
            pack(back_send.at[g, j], [code(through(own_t, own_a, state_now)), grad_pair])
            back_copy(g, j).start()
        else:
            ends[g, j, 1] = grad_now

    def back_stage(b, g):
        def taken(j):
            back_copy(g, j).wait_recv()
            ref = back_recv.at[g, j]
            pairs = [unpack(ref, index) for index in range(2)]
            return pairs + [decode(pair) for pair in pairs]

        @pl.when(z == n - 1 - b)
        def _():
            for j in ups:
                give_up(g, j, n - 1 - b, *taken(j))

        @pl.when(z == b)
        def _():
            for j in downs:
                give_down(g, j, b, *taken(j))

    def at(delay, stage):
        g = t - delay

        @pl.when((g >= 0) & (g < groups))
        def _():
            stage(g)

    reduce_at, scan_at, back_at, grad_at = schedule(n, rounds)
    def at_batch(delay, stage):
        batch = (t - delay) // units

        @pl.when((t >= delay) & (lax.rem(t - delay + units, units) == 0) & (batch < batches))
        def _():
            stage(batch)

    @pl.when((lax.rem(t, EVERY) == 0) & (t < batches * EVERY))
    def _():
        local_stage(t // EVERY)

    at_batch(grad_at + units - 1, grad_stage)
    for b in range(n - 1, 0, -1):
        at(back_at[b], functools.partial(back_stage, b))
    for r in range(rounds - 1, -1, -1):
        at(scan_at[r], functools.partial(scan_stage, r))
    for s in range(n - 1, 0, -1):
        at(reduce_at[s], functools.partial(reduce_stage, s))

    @pl.when(t == groups + grad_at - 1)
    def _():
        db_done[...] = db_all[...].astype(BF16)
        db_copy = pltpu.make_async_copy(db_done, db_out, db_sem)
        db_copy.start()

        def finish(g, carry):
            @pl.when(z < n - 1)
            def _():
                for j in ups:
                    reduce_copy(g, j).wait_send()
                for j in downs:
                    back_copy(g, j).wait_send()

            @pl.when(z > 0)
            def _():
                for j in downs:
                    reduce_copy(g, j).wait_send()
                for j in ups:
                    back_copy(g, j).wait_send()

            @pl.when(at_end)
            def _():
                for r in range(rounds):
                    for i in range(half):
                        scan_copy(r, g, i).wait_send()

            return carry

        lax.fori_loop(0, groups, finish, 0)

        def finish_batch(batch, carry):
            for index in range(len(outs)):
                store(index, batch).wait()
            return carry

        lax.fori_loop(0, batches, finish_batch, 0)
        db_copy.wait()


def per_device(queries, key_in, values_in, strength, log_decay, d_out):
    share, heads = strength.shape
    n = lax.axis_size("head")
    rounds = lax.axis_size("ctx").bit_length() - 1
    width = queries.shape[1] // heads
    count = GROUP
    half = count // 2
    groups = heads // count
    batches = groups // BATCH
    rows = count * share
    outside = pl.BlockSpec(memory_space=pl.ANY)
    full_t = jax.ShapeDtypeStruct(queries.shape, BF16)
    dma = pltpu.SemaphoreType.DMA
    vmem = pltpu.VMEM
    narrow = vmem((groups, rows, width), F32)
    square = vmem((groups, rows, rows), F32)
    state = vmem((groups, half, width, width), F32)
    reduced = vmem((groups, count, TILE + 3 * width, width), BF16)
    returned = vmem((groups, count, TILE + 2 * width, width), BF16)
    scanned = vmem((max(rounds - 1, 1), groups, half, TILE + 3 * width, width), BF16)
    final = vmem((groups, half, TILE + width, width), BF16)
    steps = groups + schedule(n, rounds)[-1]
    dq, dk, dv, dg, ds = pl.pallas_call(
        functools.partial(layer_kernel, n, rounds),
        grid=(steps,),
        in_specs=[outside] * 6,
        out_specs=[outside] * 5,
        out_shape=[full_t] * 4 + [jax.ShapeDtypeStruct((heads, share), BF16)],
        scratch_shapes=[
            vmem((5, batches, share, BATCH * count * width), BF16), vmem((heads, share), BF16),
            vmem((4, batches, share, BATCH * count * width), BF16), vmem((heads, share), F32), vmem((heads, share), BF16),
        ] + [narrow] * 2 + [square] * 3 + [
            vmem((groups, count, 3, width, width), F32), vmem((groups, count, 2, width, width), F32),
            vmem((groups, half, 3, width, width), F32),
        ] + [state] * 4 + [reduced] * 2 + [returned] * 2 + [scanned] * 2 + [final] * 2 + [
            dma((batches, 5)), dma(()), dma((batches, 4)), dma(()),
            dma((2, groups, count)), dma((2, groups, count)), dma((2, rounds, groups, half)),
        ],
        compiler_params=pltpu.CompilerParams(
            dimension_semantics=("arbitrary",), vmem_limit_bytes=63 * 1024 * 1024,
            collective_id=0, has_side_effects=True,
        ),
        name="layer",
    )(queries, key_in, values_in, log_decay, d_out, strength.T)
    return dq, dk, dv, ds.T, dg


def solution(mesh):
    spec = P(("ctx", "head"), None)
    return jax.shard_map(
        per_device, mesh=mesh, in_specs=(spec,) * 6, out_specs=(spec,) * 5, check_vma=False
    )
```

```python
import functools

import jax
import jax.numpy as jnp
from jax import lax
from jax.experimental import pallas as pl
from jax.experimental.pallas import tpu as pltpu
from jax.sharding import PartitionSpec as P

GROUP = 2
HOP = 3
SWAP = 3
NEAR = 1
FAR = 2
EVERY = 3
BACK = 4
BATCH = 4
BASE = 2
TILE = 16
RANGE = 80.0
EPS = 1e-06
F32 = jnp.float32
BF16 = jnp.bfloat16
MESH = pl.DeviceIdType.MESH

NN = (((1,), (0,)), ((), ()))
NT = (((1,), (1,)), ((), ()))


def split(x):
    high = x.astype(BF16)
    return high, (x - high.astype(F32)).astype(BF16)


def mul(a, b, dims=NN):
    return lax.dot_general(a, b, dims, preferred_element_type=F32)


def dot3(a, b, dims=NN):
    if not isinstance(a, tuple):
        return mul(a, b[0], dims) + mul(a, b[1], dims)
    if not isinstance(b, tuple):
        return mul(a[0], b, dims) + mul(a[1], b, dims)
    return mul(a[0], b[0], dims) + (mul(a[0], b[1], dims) + mul(a[1], b[0], dims))


def dot32(a, b):
    return dot3(split(a), split(b))


def rows_of(pair, start, size):
    if not isinstance(pair, tuple):
        return pair[start : start + size]
    return tuple(part[start : start + size] for part in pair)


def grids(size):
    return (
        lax.broadcasted_iota(jnp.int32, (size, size), 0),
        lax.broadcasted_iota(jnp.int32, (size, size), 1),
    )


def code(x):
    top = jnp.max(jnp.abs(x), axis=0, keepdims=True)
    scale = (top * 1.01 + 1e-30).astype(BF16)
    return jnp.exp(x * (RANGE / scale.astype(F32))).astype(BF16), scale


def decode(pair):
    coded, scale = pair
    return jnp.log(coded.astype(F32)) * (scale.astype(F32) * (1.0 / RANGE))


def pack(ref, pairs):
    width = ref.shape[1]
    row = lax.broadcasted_iota(jnp.int32, (TILE, width), 0)
    scales = jnp.zeros((TILE, width), F32)
    for index, (coded, scale) in enumerate(pairs):
        ref[TILE + index * width : TILE + (index + 1) * width] = coded
        scales = jnp.where(row == index, scale.astype(F32), scales)
    ref[:TILE] = scales.astype(BF16)


def unpack(ref, index):
    width = ref.shape[1]
    scales = ref[:TILE].astype(F32)
    return ref[TILE + index * width : TILE + (index + 1) * width], scales[index : index + 1]


def per_span(row_values, span, like):
    rows, width = like.shape
    return jnp.broadcast_to(row_values, (rows // span, span, width)).reshape(rows, width)


def gates(g, span):
    rows, width = g.shape
    row, col = grids(rows)
    sum_mask = jnp.where((row // span == col // span) & (col <= row), 1.0, 0.0).astype(BF16)
    gamma = mul(sum_mask, g)
    spans = gamma.reshape(rows // span, span, width)
    middle = spans[:, span // 2 - 1 : span // 2]
    end = spans[:, span - 1 : span]
    centred = gamma - per_span(middle, span, gamma)
    rise = jnp.exp(centred)
    fall = jnp.exp(-centred)
    head = rise * per_span(jnp.exp(middle), span, gamma)
    tail = fall * per_span(jnp.exp(end - middle), span, gamma)
    fade = jnp.exp(end).reshape(rows // span, width)
    return rise, fall, head, tail, fade


def columns_of(table, first, count):
    heads, share = table.shape
    row, col = grids(share)
    head = lax.broadcasted_iota(jnp.int32, (heads, share), 0)
    lines = [jnp.sum(jnp.where(head == first + j, table, 0.0), axis=0, keepdims=True) for j in range(count)]
    return jnp.concatenate(
        [jnp.sum(jnp.where(row == col, line, 0.0), axis=1, keepdims=True) for line in lines], axis=0
    )


def norm_of(x):
    return lax.rsqrt(jnp.sum(x * x, axis=1, keepdims=True) + EPS)


def inverses(systems, row, col, span):
    unit = jnp.where(row == col, 1.0, 0.0)
    founds = [unit - jnp.where(row // BASE == col // BASE, x, 0.0) for x in systems]
    block = BASE
    while block < span:
        off = (row // (2 * block) == col // (2 * block)) & (row // block != col // block)
        lows = [x.astype(BF16) for x in founds]
        inner = [mul(jnp.where(off, x, 0.0).astype(BF16), y) for x, y in zip(systems, lows)]
        founds = [x - mul(y, z.astype(BF16)) for x, y, z in zip(founds, lows, inner)]
        block *= 2
    lows = [x.astype(BF16) for x in founds]
    rests = [unit - y.astype(F32) - dot3(split(x), y) for x, y in zip(systems, lows)]
    small = [x.astype(BF16) for x in rests]
    rests = [x + mul(y, y) for x, y in zip(rests, small)]
    return [y.astype(F32) + mul(y, x.astype(BF16)) for x, y in zip(rests, lows)]


def loaded(held, index, batch, units, count):
    width = held.shape[3] // (units * count)

    def head(h):
        return held[index, batch, :, h * width : (h + 1) * width]

    return [jnp.concatenate([head(u * count + j) for j in range(count)], axis=0) for u in range(units)]


def over(fn, *lists):
    return [fn(*values) for values in zip(*lists)]


def local_part(batch, units, count, held, table, saved, tags):
    ev_ref, ek_ref, inv_ref, a_ref, sc_ref = saved
    span = held.shape[2]
    width = held.shape[3] // (units * count)
    rows = count * span
    first = batch * units
    ks, gs, qs, vs, os = (loaded(held, index, batch, units, count) for index in range(5))
    betas = columns_of(table[...].astype(F32), first * count, units * count)
    betas = [betas[u * rows : (u + 1) * rows] for u in range(units)]
    qs = over(lambda x: x.astype(F32), qs)
    ks = over(lambda x: x.astype(F32), ks)
    rises, falls, heads, tails, fades = zip(*(gates(x, span) for x in gs))
    q_units = over(lambda q: q * norm_of(q) * width ** (-0.5), qs)
    k_units = over(lambda k: k * norm_of(k), ks)
    row, col = grids(rows)
    inside = row // span == col // span
    k_falls = over(lambda k, fall: split(k * fall), k_units, falls)
    inners = over(
        lambda k, rise, k_fall: jnp.where(inside & (col < row), dot3(split(k * rise), k_fall, NT), 0.0),
        k_units, rises, k_falls,
    )
    beta_rows = over(lambda x: jnp.sum(jnp.where(row == col, x, 0.0), axis=0, keepdims=True), betas)
    systems = over(lambda inner, beta: inner * beta, inners, beta_rows)
    scores = over(
        lambda q, rise, k_fall: jnp.where(inside & (col <= row), dot3(split(q * rise), k_fall, NT), 0.0),
        q_units, rises, k_falls,
    )
    founds = inverses(systems, row, col, span)
    founds_s = over(split, founds)
    e_keys = over(lambda x, k, head: dot3(x, split(k * head)), founds_s, k_units, heads)
    e_values = over(dot3, founds_s, vs)
    w_keys = over(lambda x, beta: split(x * beta), e_keys, betas)
    w_values = over(lambda x, beta: split(x * beta), e_values, betas)
    reaches = over(lambda q, head, score, w: q * head - dot3(split(score), w), q_units, heads, scores, w_keys)
    k_tails = over(lambda k, tail: k * tail, k_units, tails)
    small_row, small_col = grids(width)
    diagonal = small_row == small_col
    for u in range(units):
        g = first + u
        a_ref[g] = inners[u].T
        sc_ref[g] = scores[u].T
        inv_ref[g] = founds[u].T
        ev_ref[g] = e_values[u]
        ek_ref[g] = e_keys[u]
    for j in range(count):
        at = j * span
        tails_t = over(lambda x: split(x[at : at + span].T), k_tails)
        reaches_t = over(lambda x: split(x[at : at + span].T), reaches)
        for u in range(units):
            g = first + u
            tags[g, j, 0] = jnp.where(diagonal, fades[u][j : j + 1], 0.0) - dot3(tails_t[u], rows_of(w_keys[u], at, span))
            tags[g, j, 1] = dot3(tails_t[u], rows_of(w_values[u], at, span))
            tags[g, j, 2] = dot3(reaches_t[u], os[u][at : at + span])


def grad_part(batch, units, count, held, table, saved, ends, db_all, done):
    ev_ref, ek_ref, inv_ref, a_ref, sc_ref = saved
    span = held.shape[2]
    width = held.shape[3] // (units * count)
    rows = count * span
    first = batch * units
    spans = range(count)
    ks, gs, qs, _, os = (loaded(held, index, batch, units, count) for index in range(5))
    betas = columns_of(table[...].astype(F32), first * count, units * count)
    betas = [betas[u * rows : (u + 1) * rows] for u in range(units)]
    numbers = [first + u for u in range(units)]
    states = [[ends[g, j, 0] for j in spans] for g in numbers]
    grads = [[ends[g, j, 1] for j in spans] for g in numbers]
    scores_t = [sc_ref[g] for g in numbers]
    inner_t = [a_ref[g] for g in numbers]
    found_t = [inv_ref[g] for g in numbers]
    e_values = [ev_ref[g] for g in numbers]
    e_keys = [ek_ref[g] for g in numbers]

    def emit(index, values):
        for u, value in enumerate(values):
            for j in spans:
                at = (u * count + j) * width
                done[index, batch, :, at : at + width] = value[j * span : (j + 1) * span].astype(BF16)

    qs = over(lambda x: x.astype(F32), qs)
    ks = over(lambda x: x.astype(F32), ks)
    rises, falls, heads, tails, fades = zip(*(gates(x, span) for x in gs))
    q_norms = over(norm_of, qs)
    k_norms = over(norm_of, ks)
    q_units = over(lambda q, norm: q * norm * width ** (-0.5), qs, q_norms)
    k_units = over(lambda k, norm: k * norm, ks, k_norms)
    row, col = grids(rows)
    inside = row // span == col // span
    states_s = [over(split, x) for x in states]
    grads_s = [over(split, x) for x in grads]

    def each(fn):
        return jnp.concatenate([fn(j, j * span) for j in spans], axis=0)

    def cut(x, at):
        return rows_of(x, at, span)

    e_keys = over(split, e_keys)
    k_tails = over(lambda k, tail: split(k * tail), k_units, tails)
    errors = over(lambda ev, ek, state: ev - each(lambda j, at: dot3(cut(ek, at), state[j])), e_values, e_keys, states_s)
    updates = over(lambda x, beta: split(x * beta), errors, betas)
    d_updates = over(
        lambda score, o, tail, grad: dot3(split(score), o) + each(lambda j, at: dot3(cut(tail, at), grad[j])),
        scores_t, os, k_tails, grads_s,
    )
    d_values = over(lambda x, d, beta: dot3(split(x), split(d * beta)), found_t, d_updates, betas)
    emit(0, d_values)
    d_values = over(split, d_values)
    residues = over(lambda d, a, value: d - dot3(split(a), value), d_updates, inner_t, d_values)
    d_betas = over(lambda x, y: jnp.sum(x * y, axis=1, keepdims=True), errors, residues)
    at_row, at_col = grids(span)
    sublane = lax.broadcasted_iota(jnp.int32, db_all.shape, 0)
    table_now = db_all[...]
    for u in range(units):
        for j in spans:
            piece = d_betas[u][j * span : (j + 1) * span]
            line = jnp.sum(jnp.where(at_row == at_col, piece, 0.0), axis=0, keepdims=True)
            table_now = jnp.where(sublane == (first + u) * count + j, line, table_now)
    db_all[...] = table_now
    dq_heads = over(lambda o, state: each(lambda j, at: dot3(cut(o, at), state[j], NT)), os, states_s)
    dk_heads = over(lambda d, state: -each(lambda j, at: dot3(cut(d, at), state[j], NT)), d_values, states_s)
    dk_tails = over(lambda x, grad: each(lambda j, at: dot3(cut(x, at), grad[j], NT)), updates, grads_s)
    d_scores = over(lambda o, x: jnp.where(inside & (col <= row), dot3(o, x, NT), 0.0), os, updates)
    d_inners = over(lambda d, x: jnp.where(inside & (col < row), -dot3(d, x, NT), 0.0), d_values, updates)
    k_falls = over(lambda k, fall: split(k * fall), k_units, falls)
    dq_rises = over(lambda x, y: dot3(split(x), y), d_scores, k_falls)
    dk_rises = over(lambda x, y: dot3(split(x), y), d_inners, k_falls)
    dk_falls = over(
        lambda x, y, q, k, rise: dot3(split(x.T), split(q * rise)) + dot3(split(y.T), split(k * rise)),
        d_scores, d_inners, q_units, k_units, rises,
    )
    dq_units = over(lambda x, rise, y, head: x * rise + y * head, dq_rises, rises, dq_heads, heads)
    ups = over(lambda x, rise, y, head: x * rise + y * head, dk_rises, rises, dk_heads, heads)
    tail_parts = over(lambda x, tail: x * tail, dk_tails, tails)
    downs = over(lambda x, fall, y: x * fall + y, dk_falls, falls, tail_parts)
    d_gammas = over(lambda q, dq, k, up, down: q * dq + k * (up - down), q_units, dq_units, k_units, ups, downs)
    tail_sums = over(lambda k, x: jnp.sum((k * x).reshape(count, span, width), axis=1, keepdims=True), k_units, tail_parts)
    small_row, small_col = grids(width)
    diagonal = small_row == small_col

    def at_last(state, grad, fade):
        last = []
        for j in spans:
            d_fade = jnp.sum(state[j] * grad[j], axis=1, keepdims=True)
            d_fade = jnp.sum(jnp.where(diagonal, d_fade, 0.0), axis=0, keepdims=True)
            last.append((d_fade * fade[j : j + 1]).reshape(1, 1, width))
        return jnp.concatenate(last, axis=0)

    lasts = over(at_last, states, grads, fades)
    sum_mask = jnp.where(inside & (col >= row), 1.0, 0.0).astype(BF16)
    d_decays = over(
        lambda x, tail, last: dot3(sum_mask, split(x)) + per_span(tail + last, span, x), d_gammas, tail_sums, lasts
    )
    scale = width ** (-0.5)
    emit(1, over(
        lambda d, q, norm: (d - q * (norm * norm * jnp.sum(q * d, axis=1, keepdims=True))) * (norm * scale),
        dq_units, qs, q_norms,
    ))
    dk_units = over(lambda x, y: x + y, ups, downs)
    emit(2, over(
        lambda d, k, norm: (d - k * (norm * norm * jnp.sum(k * d, axis=1, keepdims=True))) * norm,
        dk_units, ks, k_norms,
    ))
    emit(3, d_decays)


def merged(low, high):
    low_t, low_a, low_g = low
    high_t, high_a, high_g = high
    low_t_s, high_t_s = split(low_t), split(high_t)
    return (
        dot3(high_t_s, low_t_s),
        dot3(high_t_s, split(low_a)) + high_a,
        low_g + dot3(split(low_t.T), split(high_g)),
    )


def through(transfer, add, state):
    return dot32(transfer, state) + add


def through_back(transfer, add, grad):
    return dot32(transfer.T, grad) + add


def schedule(n, rounds):
    reduce_at = [HOP * s for s in range(n)]
    scan_at = []
    for r in range(rounds):
        slack = NEAR if r == 0 else FAR if r == rounds - 1 else SWAP
        scan_at.append((scan_at[-1] if r else reduce_at[-1]) + slack)
    back_at = [scan_at[-1] + BACK * b for b in range(n)]
    return reduce_at, scan_at, back_at, back_at[-1] + 1


def layer_kernel(n, rounds, q_ref, k_ref, v_ref, g_ref, o_ref, b_ref, dq_out, dk_out, dv_out, dg_out, db_out,
                 held, table, done, db_all, db_done, ev, ek, inv, a, sc, tags, ends, tot, lead, trail, state, dstate,
                 red_send, red_recv, back_send, back_recv, scan_send, scan_recv, last_send, last_recv,
                 in_sem, table_sem, out_sem, db_sem, red_sems, back_sems, scan_sems):
    t = pl.program_id(0)
    groups, count, _, width, _ = tags.shape
    batches = held.shape[1]
    units = groups // batches
    half = count // 2
    ups = range(half, count)
    downs = range(half)
    z = lax.axis_index("head")
    me = lax.axis_index("ctx")
    above = lax.rem(z + 1, n)
    below = lax.rem(z + n - 1, n)
    saved = (ev, ek, inv, a, sc)
    ins = (k_ref, g_ref, q_ref, v_ref, o_ref)
    outs = (dv_out, dq_out, dk_out, dg_out)

    def columns(batch):
        size = units * count * width
        return pl.ds(pl.multiple_of(batch * size, size), size)

    def load(index, batch):
        return pltpu.make_async_copy(ins[index].at[:, columns(batch)], held.at[index, batch], in_sem.at[batch, index])

    def store(index, batch):
        return pltpu.make_async_copy(done.at[index, batch], outs[index].at[:, columns(batch)], out_sem.at[batch, index])

    def reduce_copy(g, j):
        return pltpu.make_async_remote_copy(
            src_ref=red_send.at[g, j], dst_ref=red_recv.at[g, j], send_sem=red_sems.at[0, g, j],
            recv_sem=red_sems.at[1, g, j], device_id={"head": above if j >= half else below}, device_id_type=MESH,
        )

    def back_copy(g, j):
        return pltpu.make_async_remote_copy(
            src_ref=back_send.at[g, j], dst_ref=back_recv.at[g, j], send_sem=back_sems.at[0, g, j],
            recv_sem=back_sems.at[1, g, j], device_id={"head": below if j >= half else above}, device_id_type=MESH,
        )

    def partner(r):
        bit = 2**r
        return me + bit - 2 * bit * lax.rem(me // bit, 2)

    def upper(r):
        return lax.rem(me // 2**r, 2) == 1

    def scan_copy(r, g, i):
        final = r == rounds - 1
        source, target = (last_send, last_recv) if final else (scan_send.at[r], scan_recv.at[r])
        return pltpu.make_async_remote_copy(
            src_ref=source.at[g, i], dst_ref=target.at[g, i], send_sem=scan_sems.at[0, r, g, i],
            recv_sem=scan_sems.at[1, r, g, i], device_id={"ctx": partner(r)}, device_id_type=MESH,
        )

    at_end = (z == 0) | (z == n - 1)

    @pl.when(t == 0)
    def _():
        def start_load(batch, carry):
            for index in range(len(ins)):
                load(index, batch).start()
            return carry

        lax.fori_loop(0, batches, start_load, 0)
        pltpu.make_async_copy(b_ref, table, table_sem).start()
        barrier = pltpu.get_barrier_semaphore()

        @pl.when(z > 0)
        def _():
            pl.semaphore_signal(barrier, inc=1, device_id={"head": below}, device_id_type=MESH)

        @pl.when(z < n - 1)
        def _():
            pl.semaphore_signal(barrier, inc=1, device_id={"head": above}, device_id_type=MESH)

        for r in range(rounds):
            pl.semaphore_signal(barrier, inc=1, device_id={"ctx": partner(r)}, device_id_type=MESH)
        db_all[...] = jnp.zeros_like(db_all)
        pltpu.make_async_copy(b_ref, table, table_sem).wait()

    def own(g, j):
        return tuple(tags[g, j, index] for index in range(3))

    def received(g, j):
        ref = red_recv.at[g, j]
        return tuple(decode(unpack(ref, index)) for index in range(3))

    def send_reduced(g, j, values):
        pack(red_send.at[g, j], [code(x) for x in values])
        reduce_copy(g, j).start()

    def begin_scan(g, i, values):
        for index in range(3):
            tot[g, i, index] = values[index]
        send_scan(0, g, i, values)

    def send_scan(r, g, i, values):
        if r < rounds - 1:
            pack(scan_send.at[r, g, i], [code(x) for x in values])
        else:
            pack(last_send.at[g, i], [code(jnp.where(upper(r), values[2], values[1]))])
        scan_copy(r, g, i).start()

    def local_stage(batch):
        for index in range(len(ins)):
            load(index, batch).wait()
        local_part(batch, units, count, held, table, saved, tags)

        @pl.when(t == 0)
        def _():
            barrier = pltpu.get_barrier_semaphore()
            pl.semaphore_wait(barrier, rounds + jnp.where(z > 0, 1, 0) + jnp.where(z < n - 1, 1, 0))

        @pl.when(z == 0)
        def _():
            for u in range(units):
                for j in ups:
                    send_reduced(batch * units + u, j, own(batch * units + u, j))

        @pl.when(z == n - 1)
        def _():
            for u in range(units):
                for j in downs:
                    send_reduced(batch * units + u, j, own(batch * units + u, j))

    def grad_stage(batch):
        grad_part(batch, units, count, held, table, saved, ends, db_all, done)
        for index in range(len(outs)):
            store(index, batch).start()

    def reduce_stage(s, g):
        @pl.when(z == s)
        def _():
            for j in ups:
                reduce_copy(g, j).wait_recv()
                values = merged(received(g, j), own(g, j))
                if s < n - 1:
                    send_reduced(g, j, values)
                else:
                    begin_scan(g, j - half, values)

        @pl.when(z == n - 1 - s)
        def _():
            for j in downs:
                reduce_copy(g, j).wait_recv()
                values = merged(own(g, j), received(g, j))
                if s < n - 1:
                    send_reduced(g, j, values)
                else:
                    begin_scan(g, j, values)

    def scan_stage(r, g):
        more = r < rounds - 1

        @pl.when(at_end & upper(r))
        def _():
            for i in range(half):
                scan_copy(r, g, i).wait_recv()
                if more:
                    ref = scan_recv.at[r, g, i]
                    other, other_ends, other_grad = (decode(unpack(ref, index)) for index in range(3))
                else:
                    other_ends = decode(unpack(last_recv.at[g, i], 0))
                if r == 0:
                    state[g, i] = other_ends
                    dstate[g, i] = jnp.zeros((width, width), F32)
                else:
                    lead_s = split(lead[g, i])
                    state[g, i] = state[g, i] + dot3(lead_s, split(other_ends))
                if more:
                    if r == 0:
                        lead[g, i] = other
                        row, col = grids(width)
                        trail[g, i] = jnp.where(row == col, 1.0, 0.0)
                    else:
                        lead[g, i] = dot3(lead_s, split(other))
                    values = merged((other, other_ends, other_grad), tuple(tot[g, i, index] for index in range(3)))
                    for index in range(3):
                        tot[g, i, index] = values[index]
                    send_scan(r + 1, g, i, values)

        @pl.when(at_end & jnp.logical_not(upper(r)))
        def _():
            for i in range(half):
                scan_copy(r, g, i).wait_recv()
                if more:
                    ref = scan_recv.at[r, g, i]
                    other, other_ends, other_grad = (decode(unpack(ref, index)) for index in range(3))
                else:
                    other_grad = decode(unpack(last_recv.at[g, i], 0))
                if r == 0:
                    dstate[g, i] = other_grad
                    state[g, i] = jnp.zeros((width, width), F32)
                else:
                    trail_s = split(trail[g, i])
                    dstate[g, i] = dstate[g, i] + dot3(trail_s, split(other_grad))
                if more:
                    if r == 0:
                        trail[g, i] = other.T
                        row, col = grids(width)
                        lead[g, i] = jnp.where(row == col, 1.0, 0.0)
                    else:
                        trail[g, i] = dot3(trail_s, split(other), NT)
                    values = merged(tuple(tot[g, i, index] for index in range(3)), (other, other_ends, other_grad))
                    for index in range(3):
                        tot[g, i, index] = values[index]
                    send_scan(r + 1, g, i, values)

        if not more:
            @pl.when(z == n - 1)
            def _():
                for j in ups:
                    give_up(g, j, n - 1, code(state[g, j - half]), code(dstate[g, j - half]),
                            state[g, j - half], dstate[g, j - half])

            @pl.when(z == 0)
            def _():
                for j in downs:
                    give_down(g, j, 0, code(state[g, j]), code(dstate[g, j]), state[g, j], dstate[g, j])

    def give_up(g, j, level, state_pair, grad_pair, state_now, grad_now):
        own_t, _, own_g = own(g, j)
        ends[g, j, 1] = grad_now
        if level > 0:
            low_t, low_a, _ = received(g, j)
            ends[g, j, 0] = through(low_t, low_a, state_now)
            pack(back_send.at[g, j], [state_pair, code(through_back(own_t, own_g, grad_now))])
            back_copy(g, j).start()
        else:
            ends[g, j, 0] = state_now

    def give_down(g, j, level, state_pair, grad_pair, state_now, grad_now):
        own_t, own_a, _ = own(g, j)
        ends[g, j, 0] = state_now
        if level < n - 1:
            high_t, _, high_g = received(g, j)
            ends[g, j, 1] = through_back(high_t, high_g, grad_now)
            pack(back_send.at[g, j], [code(through(own_t, own_a, state_now)), grad_pair])
            back_copy(g, j).start()
        else:
            ends[g, j, 1] = grad_now

    def back_stage(b, g):
        def taken(j):
            back_copy(g, j).wait_recv()
            ref = back_recv.at[g, j]
            pairs = [unpack(ref, index) for index in range(2)]
            return pairs + [decode(pair) for pair in pairs]

        @pl.when(z == n - 1 - b)
        def _():
            for j in ups:
                give_up(g, j, n - 1 - b, *taken(j))

        @pl.when(z == b)
        def _():
            for j in downs:
                give_down(g, j, b, *taken(j))

    def at(delay, stage):
        g = t - delay

        @pl.when((g >= 0) & (g < groups))
        def _():
            stage(g)

    reduce_at, scan_at, back_at, grad_at = schedule(n, rounds)
    def at_batch(delay, stage):
        batch = (t - delay) // units

        @pl.when((t >= delay) & (lax.rem(t - delay + units, units) == 0) & (batch < batches))
        def _():
            stage(batch)

    @pl.when((lax.rem(t, EVERY) == 0) & (t < batches * EVERY))
    def _():
        local_stage(t // EVERY)

    at_batch(grad_at + units - 1, grad_stage)
    for b in range(n - 1, 0, -1):
        at(back_at[b], functools.partial(back_stage, b))
    for r in range(rounds - 1, -1, -1):
        at(scan_at[r], functools.partial(scan_stage, r))
    for s in range(n - 1, 0, -1):
        at(reduce_at[s], functools.partial(reduce_stage, s))

    @pl.when(t == groups + grad_at - 1)
    def _():
        db_done[...] = db_all[...].astype(BF16)
        db_copy = pltpu.make_async_copy(db_done, db_out, db_sem)
        db_copy.start()

        def finish(g, carry):
            @pl.when(z < n - 1)
            def _():
                for j in ups:
                    reduce_copy(g, j).wait_send()
                for j in downs:
                    back_copy(g, j).wait_send()

            @pl.when(z > 0)
            def _():
                for j in downs:
                    reduce_copy(g, j).wait_send()
                for j in ups:
                    back_copy(g, j).wait_send()

            @pl.when(at_end)
            def _():
                for r in range(rounds):
                    for i in range(half):
                        scan_copy(r, g, i).wait_send()

            return carry

        lax.fori_loop(0, groups, finish, 0)

        def finish_batch(batch, carry):
            for index in range(len(outs)):
                store(index, batch).wait()
            return carry

        lax.fori_loop(0, batches, finish_batch, 0)
        db_copy.wait()


def copy_kernel(*refs):
    total = len(refs) - 2
    arrays = total // 3
    sources, targets, buffers = refs[:arrays], refs[arrays : 2 * arrays], refs[2 * arrays : total]
    in_sem, out_sem = refs[total:]
    fetch = [pltpu.make_async_copy(x, y, in_sem.at[i]) for i, (x, y) in enumerate(zip(sources, buffers))]
    put = [pltpu.make_async_copy(x, y, out_sem.at[i]) for i, (x, y) in enumerate(zip(buffers, targets))]
    for copy in fetch:
        copy.start()
    for first, second in zip(fetch, put):
        first.wait()
        second.start()
    for copy in put:
        copy.wait()


def placed(arrays):
    outside = pl.BlockSpec(memory_space=pl.ANY)
    count = len(arrays)
    return pl.pallas_call(
        copy_kernel,
        in_specs=[outside] * count,
        out_specs=[outside] * count,
        out_shape=[jax.ShapeDtypeStruct(x.shape, x.dtype) for x in arrays],
        scratch_shapes=[pltpu.VMEM(x.shape, x.dtype) for x in arrays] + [pltpu.SemaphoreType.DMA((count,))] * 2,
        name="place",
    )(*arrays)


def per_device(queries, key_in, values_in, strength, log_decay, d_out):
    share, heads = strength.shape
    n = lax.axis_size("head")
    rounds = lax.axis_size("ctx").bit_length() - 1
    width = queries.shape[1] // heads
    count = GROUP
    half = count // 2
    groups = heads // count
    batches = groups // BATCH
    rows = count * share
    outside = pl.BlockSpec(memory_space=pl.ANY)
    full_t = jax.ShapeDtypeStruct(queries.shape, BF16)
    dma = pltpu.SemaphoreType.DMA
    vmem = pltpu.VMEM
    narrow = vmem((groups, rows, width), F32)
    square = vmem((groups, rows, rows), F32)
    state = vmem((groups, half, width, width), F32)
    reduced = vmem((groups, count, TILE + 3 * width, width), BF16)
    returned = vmem((groups, count, TILE + 2 * width, width), BF16)
    scanned = vmem((max(rounds - 1, 1), groups, half, TILE + 3 * width, width), BF16)
    final = vmem((groups, half, TILE + width, width), BF16)
    steps = groups + schedule(n, rounds)[-1]
    dq, dk, dv, dg, ds = pl.pallas_call(
        functools.partial(layer_kernel, n, rounds),
        grid=(steps,),
        in_specs=[outside] * 6,
        out_specs=[outside] * 5,
        out_shape=[full_t] * 4 + [jax.ShapeDtypeStruct((heads, share), BF16)],
        scratch_shapes=[
            vmem((5, batches, share, BATCH * count * width), BF16), vmem((heads, share), BF16),
            vmem((4, batches, share, BATCH * count * width), BF16), vmem((heads, share), F32), vmem((heads, share), BF16),
        ] + [narrow] * 2 + [square] * 3 + [
            vmem((groups, count, 3, width, width), F32), vmem((groups, count, 2, width, width), F32),
            vmem((groups, half, 3, width, width), F32),
        ] + [state] * 4 + [reduced] * 2 + [returned] * 2 + [scanned] * 2 + [final] * 2 + [
            dma((batches, 5)), dma(()), dma((batches, 4)), dma(()),
            dma((2, groups, count)), dma((2, groups, count)), dma((2, rounds, groups, half)),
        ],
        compiler_params=pltpu.CompilerParams(
            dimension_semantics=("arbitrary",), vmem_limit_bytes=63 * 1024 * 1024,
            collective_id=0, has_side_effects=True,
        ),
        name="layer",
    )(queries, key_in, values_in, log_decay, d_out, strength.T)
    dq, dk, dv, dg, ds = placed([dq, dk, dv, dg, ds])
    return dq, dk, dv, ds.T, dg


def solution(mesh):
    spec = P(("ctx", "head"), None)
    return jax.shard_map(
        per_device, mesh=mesh, in_specs=(spec,) * 6, out_specs=(spec,) * 5, check_vma=False
    )
```

```python
import functools

import jax
import jax.numpy as jnp
from jax import lax
from jax.experimental import pallas as pl
from jax.experimental.pallas import tpu as pltpu
from jax.sharding import PartitionSpec as P

GROUP = 2
HOP = 3
SWAP = 3
NEAR = 1
FAR = 2
EVERY = 3
BACK = 4
BATCH = 4
BASE = 2
TILE = 16
RANGE = 80.0
EPS = 1e-06
F32 = jnp.float32
BF16 = jnp.bfloat16
MESH = pl.DeviceIdType.MESH

NN = (((1,), (0,)), ((), ()))
NT = (((1,), (1,)), ((), ()))


def split(x):
    high = x.astype(BF16)
    return high, (x - high.astype(F32)).astype(BF16)


def mul(a, b, dims=NN):
    return lax.dot_general(a, b, dims, preferred_element_type=F32)


def dot3(a, b, dims=NN):
    if not isinstance(a, tuple):
        return mul(a, b[0], dims) + mul(a, b[1], dims)
    if not isinstance(b, tuple):
        return mul(a[0], b, dims) + mul(a[1], b, dims)
    return mul(a[0], b[0], dims) + (mul(a[0], b[1], dims) + mul(a[1], b[0], dims))


def dot32(a, b):
    return dot3(split(a), split(b))


def rows_of(pair, start, size):
    if not isinstance(pair, tuple):
        return pair[start : start + size]
    return tuple(part[start : start + size] for part in pair)


def grids(size):
    return (
        lax.broadcasted_iota(jnp.int32, (size, size), 0),
        lax.broadcasted_iota(jnp.int32, (size, size), 1),
    )


def code(x):
    top = jnp.max(jnp.abs(x), axis=0, keepdims=True)
    scale = (top * 1.01 + 1e-30).astype(BF16)
    return jnp.exp(x * (RANGE / scale.astype(F32))).astype(BF16), scale


def decode(pair):
    coded, scale = pair
    return jnp.log(coded.astype(F32)) * (scale.astype(F32) * (1.0 / RANGE))


def pack(ref, pairs):
    width = ref.shape[1]
    row = lax.broadcasted_iota(jnp.int32, (TILE, width), 0)
    scales = jnp.zeros((TILE, width), F32)
    for index, (coded, scale) in enumerate(pairs):
        ref[TILE + index * width : TILE + (index + 1) * width] = coded
        scales = jnp.where(row == index, scale.astype(F32), scales)
    ref[:TILE] = scales.astype(BF16)


def unpack(ref, index):
    width = ref.shape[1]
    scales = ref[:TILE].astype(F32)
    return ref[TILE + index * width : TILE + (index + 1) * width], scales[index : index + 1]


def per_span(row_values, span, like):
    rows, width = like.shape
    return jnp.broadcast_to(row_values, (rows // span, span, width)).reshape(rows, width)


def gates(g, span):
    rows, width = g.shape
    row, col = grids(rows)
    sum_mask = jnp.where((row // span == col // span) & (col <= row), 1.0, 0.0).astype(BF16)
    gamma = mul(sum_mask, g)
    spans = gamma.reshape(rows // span, span, width)
    middle = spans[:, span // 2 - 1 : span // 2]
    end = spans[:, span - 1 : span]
    centred = gamma - per_span(middle, span, gamma)
    rise = jnp.exp(centred)
    fall = jnp.exp(-centred)
    head = rise * per_span(jnp.exp(middle), span, gamma)
    tail = fall * per_span(jnp.exp(end - middle), span, gamma)
    fade = jnp.exp(end).reshape(rows // span, width)
    return rise, fall, head, tail, fade


def columns_of(table, first, count):
    heads, share = table.shape
    row, col = grids(share)
    head = lax.broadcasted_iota(jnp.int32, (heads, share), 0)
    lines = [jnp.sum(jnp.where(head == first + j, table, 0.0), axis=0, keepdims=True) for j in range(count)]
    return jnp.concatenate(
        [jnp.sum(jnp.where(row == col, line, 0.0), axis=1, keepdims=True) for line in lines], axis=0
    )


def norm_of(x):
    return lax.rsqrt(jnp.sum(x * x, axis=1, keepdims=True) + EPS)


def inverses(systems, row, col, span):
    unit = jnp.where(row == col, 1.0, 0.0)
    founds = [unit - jnp.where(row // BASE == col // BASE, x, 0.0) for x in systems]
    block = BASE
    while block < span:
        off = (row // (2 * block) == col // (2 * block)) & (row // block != col // block)
        lows = [x.astype(BF16) for x in founds]
        inner = [mul(jnp.where(off, x, 0.0).astype(BF16), y) for x, y in zip(systems, lows)]
        founds = [x - mul(y, z.astype(BF16)) for x, y, z in zip(founds, lows, inner)]
        block *= 2
    lows = [x.astype(BF16) for x in founds]
    rests = [unit - y.astype(F32) - dot3(split(x), y) for x, y in zip(systems, lows)]
    small = [x.astype(BF16) for x in rests]
    rests = [x + mul(y, y) for x, y in zip(rests, small)]
    return [y.astype(F32) + mul(y, x.astype(BF16)) for x, y in zip(rests, lows)]


def loaded(held, index, batch, units, count):
    width = held.shape[3] // (units * count)

    def head(h):
        return held[index, batch, :, h * width : (h + 1) * width]

    return [jnp.concatenate([head(u * count + j) for j in range(count)], axis=0) for u in range(units)]


def over(fn, *lists):
    return [fn(*values) for values in zip(*lists)]


def local_part(batch, units, count, held, table, saved, tags):
    ev_ref, ek_ref, inv_ref, a_ref, sc_ref = saved
    span = held.shape[2]
    width = held.shape[3] // (units * count)
    rows = count * span
    first = batch * units
    ks, gs, qs, vs, os = (loaded(held, index, batch, units, count) for index in range(5))
    betas = columns_of(table[...].astype(F32), first * count, units * count)
    betas = [betas[u * rows : (u + 1) * rows] for u in range(units)]
    qs = over(lambda x: x.astype(F32), qs)
    ks = over(lambda x: x.astype(F32), ks)
    rises, falls, heads, tails, fades = zip(*(gates(x, span) for x in gs))
    q_units = over(lambda q: q * norm_of(q) * width ** (-0.5), qs)
    k_units = over(lambda k: k * norm_of(k), ks)
    row, col = grids(rows)
    inside = row // span == col // span
    k_falls = over(lambda k, fall: split(k * fall), k_units, falls)
    inners = over(
        lambda k, rise, k_fall: jnp.where(inside & (col < row), dot3(split(k * rise), k_fall, NT), 0.0),
        k_units, rises, k_falls,
    )
    beta_rows = over(lambda x: jnp.sum(jnp.where(row == col, x, 0.0), axis=0, keepdims=True), betas)
    systems = over(lambda inner, beta: inner * beta, inners, beta_rows)
    scores = over(
        lambda q, rise, k_fall: jnp.where(inside & (col <= row), dot3(split(q * rise), k_fall, NT), 0.0),
        q_units, rises, k_falls,
    )
    founds = inverses(systems, row, col, span)
    founds_s = over(split, founds)
    e_keys = over(lambda x, k, head: dot3(x, split(k * head)), founds_s, k_units, heads)
    e_values = over(dot3, founds_s, vs)
    w_keys = over(lambda x, beta: split(x * beta), e_keys, betas)
    w_values = over(lambda x, beta: split(x * beta), e_values, betas)
    reaches = over(lambda q, head, score, w: q * head - dot3(split(score), w), q_units, heads, scores, w_keys)
    k_tails = over(lambda k, tail: k * tail, k_units, tails)
    small_row, small_col = grids(width)
    diagonal = small_row == small_col
    for u in range(units):
        g = first + u
        a_ref[g] = inners[u].T
        sc_ref[g] = scores[u].T
        inv_ref[g] = founds[u].T
        ev_ref[g] = e_values[u]
        ek_ref[g] = e_keys[u]
    for j in range(count):
        at = j * span
        tails_t = over(lambda x: split(x[at : at + span].T), k_tails)
        reaches_t = over(lambda x: split(x[at : at + span].T), reaches)
        for u in range(units):
            g = first + u
            tags[g, j, 0] = jnp.where(diagonal, fades[u][j : j + 1], 0.0) - dot3(tails_t[u], rows_of(w_keys[u], at, span))
            tags[g, j, 1] = dot3(tails_t[u], rows_of(w_values[u], at, span))
            tags[g, j, 2] = dot3(reaches_t[u], os[u][at : at + span])


def grad_part(batch, units, count, held, table, saved, ends, db_all, done):
    ev_ref, ek_ref, inv_ref, a_ref, sc_ref = saved
    span = held.shape[2]
    width = held.shape[3] // (units * count)
    rows = count * span
    first = batch * units
    spans = range(count)
    ks, gs, qs, _, os = (loaded(held, index, batch, units, count) for index in range(5))
    betas = columns_of(table[...].astype(F32), first * count, units * count)
    betas = [betas[u * rows : (u + 1) * rows] for u in range(units)]
    numbers = [first + u for u in range(units)]
    states = [[ends[g, j, 0] for j in spans] for g in numbers]
    grads = [[ends[g, j, 1] for j in spans] for g in numbers]
    scores_t = [sc_ref[g] for g in numbers]
    inner_t = [a_ref[g] for g in numbers]
    found_t = [inv_ref[g] for g in numbers]
    e_values = [ev_ref[g] for g in numbers]
    e_keys = [ek_ref[g] for g in numbers]

    def emit(index, values):
        for u, value in enumerate(values):
            for j in spans:
                at = (u * count + j) * width
                done[index, batch, :, at : at + width] = value[j * span : (j + 1) * span].astype(BF16)

    qs = over(lambda x: x.astype(F32), qs)
    ks = over(lambda x: x.astype(F32), ks)
    rises, falls, heads, tails, fades = zip(*(gates(x, span) for x in gs))
    q_norms = over(norm_of, qs)
    k_norms = over(norm_of, ks)
    q_units = over(lambda q, norm: q * norm * width ** (-0.5), qs, q_norms)
    k_units = over(lambda k, norm: k * norm, ks, k_norms)
    row, col = grids(rows)
    inside = row // span == col // span
    states_s = [over(split, x) for x in states]
    grads_s = [over(split, x) for x in grads]

    def each(fn):
        return jnp.concatenate([fn(j, j * span) for j in spans], axis=0)

    def cut(x, at):
        return rows_of(x, at, span)

    e_keys = over(split, e_keys)
    k_tails = over(lambda k, tail: split(k * tail), k_units, tails)
    errors = over(lambda ev, ek, state: ev - each(lambda j, at: dot3(cut(ek, at), state[j])), e_values, e_keys, states_s)
    updates = over(lambda x, beta: split(x * beta), errors, betas)
    d_updates = over(
        lambda score, o, tail, grad: dot3(split(score), o) + each(lambda j, at: dot3(cut(tail, at), grad[j])),
        scores_t, os, k_tails, grads_s,
    )
    d_values = over(lambda x, d, beta: dot3(split(x), split(d * beta)), found_t, d_updates, betas)
    emit(0, d_values)
    d_values = over(split, d_values)
    residues = over(lambda d, a, value: d - dot3(split(a), value), d_updates, inner_t, d_values)
    d_betas = over(lambda x, y: jnp.sum(x * y, axis=1, keepdims=True), errors, residues)
    at_row, at_col = grids(span)
    sublane = lax.broadcasted_iota(jnp.int32, db_all.shape, 0)
    table_now = db_all[...]
    for u in range(units):
        for j in spans:
            piece = d_betas[u][j * span : (j + 1) * span]
            line = jnp.sum(jnp.where(at_row == at_col, piece, 0.0), axis=0, keepdims=True)
            table_now = jnp.where(sublane == (first + u) * count + j, line, table_now)
    db_all[...] = table_now
    dq_heads = over(lambda o, state: each(lambda j, at: dot3(cut(o, at), state[j], NT)), os, states_s)
    dk_heads = over(lambda d, state: -each(lambda j, at: dot3(cut(d, at), state[j], NT)), d_values, states_s)
    dk_tails = over(lambda x, grad: each(lambda j, at: dot3(cut(x, at), grad[j], NT)), updates, grads_s)
    d_scores = over(lambda o, x: jnp.where(inside & (col <= row), dot3(o, x, NT), 0.0), os, updates)
    d_inners = over(lambda d, x: jnp.where(inside & (col < row), -dot3(d, x, NT), 0.0), d_values, updates)
    k_falls = over(lambda k, fall: split(k * fall), k_units, falls)
    dq_rises = over(lambda x, y: dot3(split(x), y), d_scores, k_falls)
    dk_rises = over(lambda x, y: dot3(split(x), y), d_inners, k_falls)
    dk_falls = over(
        lambda x, y, q, k, rise: dot3(split(x.T), split(q * rise)) + dot3(split(y.T), split(k * rise)),
        d_scores, d_inners, q_units, k_units, rises,
    )
    dq_units = over(lambda x, rise, y, head: x * rise + y * head, dq_rises, rises, dq_heads, heads)
    ups = over(lambda x, rise, y, head: x * rise + y * head, dk_rises, rises, dk_heads, heads)
    tail_parts = over(lambda x, tail: x * tail, dk_tails, tails)
    downs = over(lambda x, fall, y: x * fall + y, dk_falls, falls, tail_parts)
    d_gammas = over(lambda q, dq, k, up, down: q * dq + k * (up - down), q_units, dq_units, k_units, ups, downs)
    tail_sums = over(lambda k, x: jnp.sum((k * x).reshape(count, span, width), axis=1, keepdims=True), k_units, tail_parts)
    small_row, small_col = grids(width)
    diagonal = small_row == small_col

    def at_last(state, grad, fade):
        last = []
        for j in spans:
            d_fade = jnp.sum(state[j] * grad[j], axis=1, keepdims=True)
            d_fade = jnp.sum(jnp.where(diagonal, d_fade, 0.0), axis=0, keepdims=True)
            last.append((d_fade * fade[j : j + 1]).reshape(1, 1, width))
        return jnp.concatenate(last, axis=0)

    lasts = over(at_last, states, grads, fades)
    sum_mask = jnp.where(inside & (col >= row), 1.0, 0.0).astype(BF16)
    d_decays = over(
        lambda x, tail, last: dot3(sum_mask, split(x)) + per_span(tail + last, span, x), d_gammas, tail_sums, lasts
    )
    scale = width ** (-0.5)
    emit(1, over(
        lambda d, q, norm: (d - q * (norm * norm * jnp.sum(q * d, axis=1, keepdims=True))) * (norm * scale),
        dq_units, qs, q_norms,
    ))
    dk_units = over(lambda x, y: x + y, ups, downs)
    emit(2, over(
        lambda d, k, norm: (d - k * (norm * norm * jnp.sum(k * d, axis=1, keepdims=True))) * norm,
        dk_units, ks, k_norms,
    ))
    emit(3, d_decays)


def merged(low, high):
    low_t, low_a, low_g = low
    high_t, high_a, high_g = high
    low_t_s, high_t_s = split(low_t), split(high_t)
    return (
        dot3(high_t_s, low_t_s),
        dot3(high_t_s, split(low_a)) + high_a,
        low_g + dot3(split(low_t.T), split(high_g)),
    )


def through(transfer, add, state):
    return dot32(transfer, state) + add


def through_back(transfer, add, grad):
    return dot32(transfer.T, grad) + add


def schedule(n, rounds):
    reduce_at = [HOP * s for s in range(n)]
    scan_at = []
    for r in range(rounds):
        slack = NEAR if r == 0 else FAR if r == rounds - 1 else SWAP
        scan_at.append((scan_at[-1] if r else reduce_at[-1]) + slack)
    back_at = [scan_at[-1] + BACK * b for b in range(n)]
    return reduce_at, scan_at, back_at, back_at[-1]


def layer_kernel(n, rounds, q_ref, k_ref, v_ref, g_ref, o_ref, b_ref, dq_out, dk_out, dv_out, dg_out, db_out,
                 held, table, done, db_all, db_done, ev, ek, inv, a, sc, tags, ends, tot, lead, trail, state, dstate,
                 red_send, red_recv, back_send, back_recv, scan_send, scan_recv, last_send, last_recv,
                 in_sem, table_sem, out_sem, db_sem, red_sems, back_sems, scan_sems):
    t = pl.program_id(0)
    groups, count, _, width, _ = tags.shape
    batches = held.shape[1]
    units = groups // batches
    half = count // 2
    ups = range(half, count)
    downs = range(half)
    z = lax.axis_index("head")
    me = lax.axis_index("ctx")
    above = lax.rem(z + 1, n)
    below = lax.rem(z + n - 1, n)
    saved = (ev, ek, inv, a, sc)
    ins = (k_ref, g_ref, q_ref, v_ref, o_ref)
    outs = (dv_out, dq_out, dk_out, dg_out)

    def columns(batch):
        size = units * count * width
        return pl.ds(pl.multiple_of(batch * size, size), size)

    def load(index, batch):
        return pltpu.make_async_copy(ins[index].at[:, columns(batch)], held.at[index, batch], in_sem.at[batch, index])

    def store(index, batch):
        return pltpu.make_async_copy(done.at[index, batch], outs[index].at[:, columns(batch)], out_sem.at[batch, index])

    def reduce_copy(g, j):
        return pltpu.make_async_remote_copy(
            src_ref=red_send.at[g, j], dst_ref=red_recv.at[g, j], send_sem=red_sems.at[0, g, j],
            recv_sem=red_sems.at[1, g, j], device_id={"head": above if j >= half else below}, device_id_type=MESH,
        )

    def back_copy(g, j):
        return pltpu.make_async_remote_copy(
            src_ref=back_send.at[g, j], dst_ref=back_recv.at[g, j], send_sem=back_sems.at[0, g, j],
            recv_sem=back_sems.at[1, g, j], device_id={"head": below if j >= half else above}, device_id_type=MESH,
        )

    def partner(r):
        bit = 2**r
        return me + bit - 2 * bit * lax.rem(me // bit, 2)

    def upper(r):
        return lax.rem(me // 2**r, 2) == 1

    def scan_copy(r, g, i):
        final = r == rounds - 1
        source, target = (last_send, last_recv) if final else (scan_send.at[r], scan_recv.at[r])
        return pltpu.make_async_remote_copy(
            src_ref=source.at[g, i], dst_ref=target.at[g, i], send_sem=scan_sems.at[0, r, g, i],
            recv_sem=scan_sems.at[1, r, g, i], device_id={"ctx": partner(r)}, device_id_type=MESH,
        )

    at_end = (z == 0) | (z == n - 1)

    @pl.when(t == 0)
    def _():
        def start_load(batch, carry):
            for index in range(len(ins)):
                load(index, batch).start()
            return carry

        lax.fori_loop(0, batches, start_load, 0)
        pltpu.make_async_copy(b_ref, table, table_sem).start()
        barrier = pltpu.get_barrier_semaphore()

        @pl.when(z > 0)
        def _():
            pl.semaphore_signal(barrier, inc=1, device_id={"head": below}, device_id_type=MESH)

        @pl.when(z < n - 1)
        def _():
            pl.semaphore_signal(barrier, inc=1, device_id={"head": above}, device_id_type=MESH)

        for r in range(rounds):
            pl.semaphore_signal(barrier, inc=1, device_id={"ctx": partner(r)}, device_id_type=MESH)
        db_all[...] = jnp.zeros_like(db_all)
        pltpu.make_async_copy(b_ref, table, table_sem).wait()

    def own(g, j):
        return tuple(tags[g, j, index] for index in range(3))

    def received(g, j):
        ref = red_recv.at[g, j]
        return tuple(decode(unpack(ref, index)) for index in range(3))

    def send_reduced(g, j, values):
        pack(red_send.at[g, j], [code(x) for x in values])
        reduce_copy(g, j).start()

    def begin_scan(g, i, values):
        for index in range(3):
            tot[g, i, index] = values[index]
        send_scan(0, g, i, values)

    def send_scan(r, g, i, values):
        if r < rounds - 1:
            pack(scan_send.at[r, g, i], [code(x) for x in values])
        else:
            pack(last_send.at[g, i], [code(jnp.where(upper(r), values[2], values[1]))])
        scan_copy(r, g, i).start()

    def local_stage(batch):
        for index in range(len(ins)):
            load(index, batch).wait()
        local_part(batch, units, count, held, table, saved, tags)

        @pl.when(t == 0)
        def _():
            barrier = pltpu.get_barrier_semaphore()
            pl.semaphore_wait(barrier, rounds + jnp.where(z > 0, 1, 0) + jnp.where(z < n - 1, 1, 0))

        @pl.when(z == 0)
        def _():
            for u in range(units):
                for j in ups:
                    send_reduced(batch * units + u, j, own(batch * units + u, j))

        @pl.when(z == n - 1)
        def _():
            for u in range(units):
                for j in downs:
                    send_reduced(batch * units + u, j, own(batch * units + u, j))

    def grad_stage(batch):
        grad_part(batch, units, count, held, table, saved, ends, db_all, done)
        for index in range(len(outs)):
            store(index, batch).start()

    def reduce_stage(s, g):
        @pl.when(z == s)
        def _():
            for j in ups:
                reduce_copy(g, j).wait_recv()
                values = merged(received(g, j), own(g, j))
                if s < n - 1:
                    send_reduced(g, j, values)
                else:
                    begin_scan(g, j - half, values)

        @pl.when(z == n - 1 - s)
        def _():
            for j in downs:
                reduce_copy(g, j).wait_recv()
                values = merged(own(g, j), received(g, j))
                if s < n - 1:
                    send_reduced(g, j, values)
                else:
                    begin_scan(g, j, values)

    def scan_stage(r, g):
        more = r < rounds - 1

        @pl.when(at_end & upper(r))
        def _():
            for i in range(half):
                scan_copy(r, g, i).wait_recv()
                if more:
                    ref = scan_recv.at[r, g, i]
                    other, other_ends, other_grad = (decode(unpack(ref, index)) for index in range(3))
                else:
                    other_ends = decode(unpack(last_recv.at[g, i], 0))
                if r == 0:
                    state[g, i] = other_ends
                    dstate[g, i] = jnp.zeros((width, width), F32)
                else:
                    lead_s = split(lead[g, i])
                    state[g, i] = state[g, i] + dot3(lead_s, split(other_ends))
                if more:
                    if r == 0:
                        lead[g, i] = other
                        row, col = grids(width)
                        trail[g, i] = jnp.where(row == col, 1.0, 0.0)
                    else:
                        lead[g, i] = dot3(lead_s, split(other))
                    values = merged((other, other_ends, other_grad), tuple(tot[g, i, index] for index in range(3)))
                    for index in range(3):
                        tot[g, i, index] = values[index]
                    send_scan(r + 1, g, i, values)

        @pl.when(at_end & jnp.logical_not(upper(r)))
        def _():
            for i in range(half):
                scan_copy(r, g, i).wait_recv()
                if more:
                    ref = scan_recv.at[r, g, i]
                    other, other_ends, other_grad = (decode(unpack(ref, index)) for index in range(3))
                else:
                    other_grad = decode(unpack(last_recv.at[g, i], 0))
                if r == 0:
                    dstate[g, i] = other_grad
                    state[g, i] = jnp.zeros((width, width), F32)
                else:
                    trail_s = split(trail[g, i])
                    dstate[g, i] = dstate[g, i] + dot3(trail_s, split(other_grad))
                if more:
                    if r == 0:
                        trail[g, i] = other.T
                        row, col = grids(width)
                        lead[g, i] = jnp.where(row == col, 1.0, 0.0)
                    else:
                        trail[g, i] = dot3(trail_s, split(other), NT)
                    values = merged(tuple(tot[g, i, index] for index in range(3)), (other, other_ends, other_grad))
                    for index in range(3):
                        tot[g, i, index] = values[index]
                    send_scan(r + 1, g, i, values)

        if not more:
            @pl.when(z == n - 1)
            def _():
                for j in ups:
                    give_up(g, j, n - 1, code(state[g, j - half]), code(dstate[g, j - half]),
                            state[g, j - half], dstate[g, j - half])

            @pl.when(z == 0)
            def _():
                for j in downs:
                    give_down(g, j, 0, code(state[g, j]), code(dstate[g, j]), state[g, j], dstate[g, j])

    def give_up(g, j, level, state_pair, grad_pair, state_now, grad_now):
        own_t, _, own_g = own(g, j)
        ends[g, j, 1] = grad_now
        if level > 0:
            low_t, low_a, _ = received(g, j)
            ends[g, j, 0] = through(low_t, low_a, state_now)
            pack(back_send.at[g, j], [state_pair, code(through_back(own_t, own_g, grad_now))])
            back_copy(g, j).start()
        else:
            ends[g, j, 0] = state_now

    def give_down(g, j, level, state_pair, grad_pair, state_now, grad_now):
        own_t, own_a, _ = own(g, j)
        ends[g, j, 0] = state_now
        if level < n - 1:
            high_t, _, high_g = received(g, j)
            ends[g, j, 1] = through_back(high_t, high_g, grad_now)
            pack(back_send.at[g, j], [code(through(own_t, own_a, state_now)), grad_pair])
            back_copy(g, j).start()
        else:
            ends[g, j, 1] = grad_now

    def back_stage(b, g):
        def taken(j):
            back_copy(g, j).wait_recv()
            ref = back_recv.at[g, j]
            pairs = [unpack(ref, index) for index in range(2)]
            return pairs + [decode(pair) for pair in pairs]

        @pl.when(z == n - 1 - b)
        def _():
            for j in ups:
                give_up(g, j, n - 1 - b, *taken(j))

        @pl.when(z == b)
        def _():
            for j in downs:
                give_down(g, j, b, *taken(j))

    def at(delay, stage):
        g = t - delay

        @pl.when((g >= 0) & (g < groups))
        def _():
            stage(g)

    reduce_at, scan_at, back_at, grad_at = schedule(n, rounds)
    def at_batch(delay, stage):
        batch = (t - delay) // units

        @pl.when((t >= delay) & (lax.rem(t - delay + units, units) == 0) & (batch < batches))
        def _():
            stage(batch)

    @pl.when((lax.rem(t, EVERY) == 0) & (t < batches * EVERY))
    def _():
        local_stage(t // EVERY)

    for s in range(n - 1, 0, -1):
        at(reduce_at[s], functools.partial(reduce_stage, s))
    for b in range(n - 1, 0, -1):
        at(back_at[b], functools.partial(back_stage, b))
    for r in range(rounds - 1, -1, -1):
        at(scan_at[r], functools.partial(scan_stage, r))
    at_batch(grad_at + units - 1, grad_stage)

    @pl.when(t == groups + grad_at - 1)
    def _():
        db_done[...] = db_all[...].astype(BF16)
        db_copy = pltpu.make_async_copy(db_done, db_out, db_sem)
        db_copy.start()

        def finish(g, carry):
            @pl.when(z < n - 1)
            def _():
                for j in ups:
                    reduce_copy(g, j).wait_send()
                for j in downs:
                    back_copy(g, j).wait_send()

            @pl.when(z > 0)
            def _():
                for j in downs:
                    reduce_copy(g, j).wait_send()
                for j in ups:
                    back_copy(g, j).wait_send()

            @pl.when(at_end)
            def _():
                for r in range(rounds):
                    for i in range(half):
                        scan_copy(r, g, i).wait_send()

            return carry

        lax.fori_loop(0, groups, finish, 0)

        def finish_batch(batch, carry):
            for index in range(len(outs)):
                store(index, batch).wait()
            return carry

        lax.fori_loop(0, batches, finish_batch, 0)
        db_copy.wait()


def copy_kernel(*refs):
    total = len(refs) - 2
    arrays = total // 3
    sources, targets, buffers = refs[:arrays], refs[arrays : 2 * arrays], refs[2 * arrays : total]
    in_sem, out_sem = refs[total:]
    fetch = [pltpu.make_async_copy(x, y, in_sem.at[i]) for i, (x, y) in enumerate(zip(sources, buffers))]
    put = [pltpu.make_async_copy(x, y, out_sem.at[i]) for i, (x, y) in enumerate(zip(buffers, targets))]
    for copy in fetch:
        copy.start()
    for first, second in zip(fetch, put):
        first.wait()
        second.start()
    for copy in put:
        copy.wait()


def placed(arrays):
    outside = pl.BlockSpec(memory_space=pl.ANY)
    count = len(arrays)
    return pl.pallas_call(
        copy_kernel,
        in_specs=[outside] * count,
        out_specs=[outside] * count,
        out_shape=[jax.ShapeDtypeStruct(x.shape, x.dtype) for x in arrays],
        scratch_shapes=[pltpu.VMEM(x.shape, x.dtype) for x in arrays] + [pltpu.SemaphoreType.DMA((count,))] * 2,
        name="place",
    )(*arrays)


def per_device(queries, key_in, values_in, strength, log_decay, d_out):
    share, heads = strength.shape
    n = lax.axis_size("head")
    rounds = lax.axis_size("ctx").bit_length() - 1
    width = queries.shape[1] // heads
    count = GROUP
    half = count // 2
    groups = heads // count
    batches = groups // BATCH
    rows = count * share
    outside = pl.BlockSpec(memory_space=pl.ANY)
    full_t = jax.ShapeDtypeStruct(queries.shape, BF16)
    dma = pltpu.SemaphoreType.DMA
    vmem = pltpu.VMEM
    narrow = vmem((groups, rows, width), F32)
    square = vmem((groups, rows, rows), F32)
    state = vmem((groups, half, width, width), F32)
    reduced = vmem((groups, count, TILE + 3 * width, width), BF16)
    returned = vmem((groups, count, TILE + 2 * width, width), BF16)
    scanned = vmem((max(rounds - 1, 1), groups, half, TILE + 3 * width, width), BF16)
    final = vmem((groups, half, TILE + width, width), BF16)
    steps = groups + schedule(n, rounds)[-1]
    dq, dk, dv, dg, ds = pl.pallas_call(
        functools.partial(layer_kernel, n, rounds),
        grid=(steps,),
        in_specs=[outside] * 6,
        out_specs=[outside] * 5,
        out_shape=[full_t] * 4 + [jax.ShapeDtypeStruct((heads, share), BF16)],
        scratch_shapes=[
            vmem((5, batches, share, BATCH * count * width), BF16), vmem((heads, share), BF16),
            vmem((4, batches, share, BATCH * count * width), BF16), vmem((heads, share), F32), vmem((heads, share), BF16),
        ] + [narrow] * 2 + [square] * 3 + [
            vmem((groups, count, 3, width, width), F32), vmem((groups, count, 2, width, width), F32),
            vmem((groups, half, 3, width, width), F32),
        ] + [state] * 4 + [reduced] * 2 + [returned] * 2 + [scanned] * 2 + [final] * 2 + [
            dma((batches, 5)), dma(()), dma((batches, 4)), dma(()),
            dma((2, groups, count)), dma((2, groups, count)), dma((2, rounds, groups, half)),
        ],
        compiler_params=pltpu.CompilerParams(
            dimension_semantics=("arbitrary",), vmem_limit_bytes=63 * 1024 * 1024,
            collective_id=0, has_side_effects=True,
        ),
        name="layer",
    )(queries, key_in, values_in, log_decay, d_out, strength.T)
    dq, dk, dv, dg, ds = placed([dq, dk, dv, dg, ds])
    return dq, dk, dv, ds.T, dg


def solution(mesh):
    spec = P(("ctx", "head"), None)
    return jax.shard_map(
        per_device, mesh=mesh, in_specs=(spec,) * 6, out_specs=(spec,) * 5, check_vma=False
    )
```
